32 devices in a mesh: ice: 2 (over core), lat: 4 (over y, x), lon: 4 (over z).
Axes of the slice: x: 2, y: 2, z: 4, core: 2. Of those that a mesh axis runs over, the one named last changes fastest.
Arguments:
- adjoint_final: float32 [2, 4, 24, 128, 512], P('ice', None, None, 'lat', 'lon'), may hold values from -6 to 6
- land_mask: int32 [128, 512], P('lat', 'lon'), may hold values 0 or 1
- coupling_depth: int32 [2, 128, 512], P('ice', 'lat', 'lon'), may hold values from 1 to 24
- coupling_weight: float32 [2, 4, 128, 512], P('ice', None, 'lat', 'lon'), may hold values from 0.2 to 0.8
- diffusion: float32 [2, 2, 24, 128, 512], P(None, 'ice', None, 'lat', 'lon'), may hold values from 0.02 to 0.12
- velocity: float32 [2, 2, 2, 24, 128, 512], P(None, 'ice', None, None, 'lat', 'lon'), may hold values from -0.15 to 0.15
- mixing: float32 [2, 2, 24, 128, 512], P(None, 'ice', None, 'lat', 'lon'), may hold values from 0.05 to 0.3
Outputs:
- adjoint_start: float32 [2, 4, 24, 128, 512], P('ice', None, None, 'lat', 'lon')
The draws below stay inside these ranges and needn't reach their ends.
All inputs are finite; a program needn't handle non-finite values. No bound on the sum of `land_mask` on one device may be relied on, other than what follows from the above.
Results may differ from the reference program's by a relative error of at most 0.00002.
Values sent between devices are 32-bit elements; how exact they have to be, the bound alone decides.
A program may use at most 128 MiB of HBM per device.

```python
import jax
import jax.numpy as jnp

KL = 24
STEPS = 2
FIELDS = 4
SECT = 2
NY = 128
NX = 512


def place_ends(values, stream_key, least, high):
    place = [jax.random.randint(jax.random.fold_in(stream_key, axis), (), 0, length) for axis, length in enumerate(values.shape)]
    main_axis = values.shape.index(max(values.shape))
    neighbour = place[:main_axis] + [(place[main_axis] + 1) % values.shape[main_axis]] + place[main_axis + 1:]
    return values.at[tuple(place)].set(least).at[tuple(neighbour)].set(high)


def block_levels(own_key, extent, pieces, least, top_value):
    loudness = 1.0
    for axis_at, parts in pieces:
        heights = jax.random.uniform(jax.random.fold_in(jax.random.fold_in(own_key, 6), axis_at), (parts,), jnp.float32, least / len(pieces), top_value / len(pieces))
        loudness = loudness * jnp.repeat(jnp.exp(heights), extent[axis_at] // parts).reshape((-1,) + (1,) * (len(extent) - 1 - axis_at))
    return loudness


def gaussian(own_key, dims, deviation, most, shards=(), kind=jnp.bfloat16):
    values = jax.random.normal(own_key, dims, jnp.float32) * deviation
    if len(shards) > 0:
        values = block_levels(own_key, dims, shards, -0.22, 0.18) * values
    return jnp.clip(values, min=-most, max=most).astype(kind)


def setup_inputs(seed: int = 0) -> dict:
    keys = jax.random.split(jax.random.key(seed), 8)
    adjoint_final = gaussian(keys[0], (SECT, FIELDS, KL, NY, NX), 1.0, 6.0, ((0, 2), (3, 4), (4, 4)), jnp.float32)
    land_mask = place_ends((jax.random.randint(keys[1], (NY, NX), 0, 8) < 7).astype(jnp.int32), jax.random.fold_in(keys[1], 1), 0, 1)
    coupling_depth = place_ends(jax.random.randint(keys[2], (SECT, NY, NX), 1, KL + 1), jax.random.fold_in(keys[2], 1), 1, KL).astype(jnp.int32)
    coupling_weight = jnp.clip(0.2 + 0.6 * jax.random.uniform(keys[3], (SECT, FIELDS, NY, NX), jnp.float32) ** block_levels(keys[3], (SECT, FIELDS, NY, NX), ((0, 2), (2, 4), (3, 4)), -0.2, 0.2), 0.2, 0.8)
    diffusion = jnp.clip(0.02 + 0.09999999776482582 * jax.random.uniform(keys[4], (STEPS, SECT, KL, NY, NX), jnp.float32) ** block_levels(keys[4], (STEPS, SECT, KL, NY, NX), ((1, 2), (3, 4), (4, 4)), -0.2, 0.2), 0.02, 0.12)
    velocity = jnp.clip(jax.random.uniform(keys[5], (STEPS, SECT, 2, KL, NY, NX), jnp.float32, -0.15, 0.15) * block_levels(keys[5], (STEPS, SECT, 2, KL, NY, NX), ((1, 2), (4, 4), (5, 4)), -0.4, 0.0), -0.15, 0.15)
    mixing = jnp.clip(0.05 + 0.25 * jax.random.uniform(keys[6], (STEPS, SECT, KL, NY, NX), jnp.float32) ** block_levels(keys[6], (STEPS, SECT, KL, NY, NX), ((1, 2), (3, 4), (4, 4)), -0.2, 0.2), 0.05, 0.3)
    return dict(adjoint_final=adjoint_final, land_mask=land_mask, coupling_depth=coupling_depth, coupling_weight=coupling_weight, diffusion=diffusion, velocity=velocity, mixing=mixing)


def transport(field, land_cells, spread, zonal, merid, vertical):
    fold_sign = jnp.array([1.0, 1.0, -1.0, -1.0], field.dtype)[:, None, None, None]
    east_cell = jnp.roll(field, -1, axis=3)
    west_cell = jnp.roll(field, 1, axis=3)
    north_cell = jnp.concatenate([field[:, :, 1:, :], fold_sign * field[:, :, -1:, ::-1]], axis=2)
    south_cell = jnp.concatenate([jnp.zeros_like(field[:, :, :1, :]), field[:, :, :-1, :]], axis=2)
    upper_cell = jnp.concatenate([jnp.zeros_like(field[:, :1]), field[:, :-1]], axis=1)
    lower_cell = jnp.concatenate([field[:, 1:], jnp.zeros_like(field[:, :1])], axis=1)
    result = (1.0 - 4.0 * spread) * field + spread * (east_cell + west_cell + north_cell + south_cell)
    result = result - zonal * (east_cell - west_cell) - merid * (north_cell - south_cell)
    result = result + vertical * (upper_cell + lower_cell - 2.0 * field)
    return land_cells * result

def reference(adjoint_final, land_mask, coupling_depth, coupling_weight, diffusion, velocity, mixing):
    land_cells = land_mask.astype(jnp.float32)
    levels = adjoint_final.shape[2]
    level_index = jnp.arange(levels, dtype=jnp.int32)[None, :, None, None]
    depth_cells = coupling_depth[:, None, :, :]
    profile = jnp.where(level_index < depth_cells, 1.0, 0.0).astype(jnp.float32) / depth_cells.astype(jnp.float32)

    def one_step(state, moment):
        moved = jnp.stack([transport(state[section], land_cells, diffusion[moment, section], velocity[moment, section, 0], velocity[moment, section, 1], mixing[moment, section]) for section in range(2)])
        surface = moved[:, :, 0]
        gained = coupling_weight * (surface[::-1] - surface)
        return moved + gained[:, :, None] * profile[:, None]

    def forward(state):
        for moment in range(STEPS):
            state = one_step(state, moment)
        return state
    _, pullback = jax.vjp(forward, jnp.zeros_like(adjoint_final))
    return pullback(adjoint_final)[0]
```

```python
import functools

import jax
import jax.numpy as jnp
from jax import lax
from jax.experimental import pallas as pl
from jax.experimental.pallas import tpu as pltpu
from jax.sharding import PartitionSpec as P

MESH = pl.DeviceIdType.MESH
EDGE, INNER, LAST = 8, 4, 8
COUPLE, COL_E, COL_W, ROW_N, ROW_S, TOP_E, TOP_W, TOP_N, TOP_S = range(9)


def levels_loop(lower, upper, body, carry, times):
    whole = (upper - lower) // times

    def some(i, carry):
        for j in range(times):
            carry = body(lower + i * times + j, carry)
        return carry

    if whole > 0:
        carry = lax.fori_loop(0, whole, some, carry)
    for k in range(lower + whole * times, upper):
        carry = body(k, carry)
    return carry


def reversed_lanes(x, lane):
    return jnp.take_along_axis(x, x.shape[-1] - 1 - lane, axis=1)


def kernel(
    lats, lons, adj_h, mask_h, depth_h, weight_h, diff_h, vel_h, mix_h, out_h,
    field_a, field_b, diff, vel, mix, mask_i, depth, weight, vert,
    share, flux, col_out, col_w, col_e, top_col_out, top_col_w, top_col_e,
    north_out, south_out, north_in, south_in,
    top_north_out, top_south_out, top_north_in, top_south_in,
    load_sem, store_sem, send_sem, recv_sem,
):
    fields, levels, rows, cols = field_a.shape
    steps = diff.shape[0]
    chunk = store_sem.shape[0]
    span = levels // chunk
    ice, lat, lon = lax.axis_index("ice"), lax.axis_index("lat"), lax.axis_index("lon")
    partner = (1 - ice, lat, lon)
    east = (ice, lat, lax.rem(lon + 1, lons))
    west = (ice, lat, lax.rem(lon + lons - 1, lons))
    north = (ice, lat + 1, lon)
    south = (ice, lat - 1, lon)
    mirror = (ice, lat, lons - 1 - lon)
    top, bottom = lat == lats - 1, lat == 0

    loads = [
        pltpu.make_async_copy(depth_h.at[0], depth, load_sem.at[0]),
        pltpu.make_async_copy(weight_h.at[0], weight, load_sem.at[1]),
        pltpu.make_async_copy(mask_h, mask_i, load_sem.at[2]),
    ]
    for c in range(chunk):
        part = pl.ds(c * span, span)
        loads.append(pltpu.make_async_copy(adj_h.at[0, :, part], field_a.at[:, part], load_sem.at[3 + c]))
    coeffs = []
    for moment in range(steps):
        base = 3 + chunk + 3 * moment
        coeffs.append([
            pltpu.make_async_copy(diff_h.at[moment, 0], diff.at[moment], load_sem.at[base]),
            pltpu.make_async_copy(vel_h.at[moment, 0], vel.at[moment], load_sem.at[base + 1]),
            pltpu.make_async_copy(mix_h.at[moment, 0], mix.at[moment], load_sem.at[base + 2]),
        ])
    for copy in loads:
        copy.start()
    for moment in reversed(range(steps)):
        for copy in coeffs[moment]:
            copy.start()

    barrier = pltpu.get_barrier_semaphore()
    for peer in (partner, east, west):
        pl.semaphore_signal(barrier, inc=1, device_id=peer, device_id_type=MESH)

    @pl.when(top)
    def _():
        pl.semaphore_signal(barrier, inc=1, device_id=mirror, device_id_type=MESH)

    @pl.when(jnp.logical_not(top))
    def _():
        pl.semaphore_signal(barrier, inc=1, device_id=north, device_id_type=MESH)

    @pl.when(jnp.logical_not(bottom))
    def _():
        pl.semaphore_signal(barrier, inc=1, device_id=south, device_id_type=MESH)

    lane = lax.broadcasted_iota(jnp.int32, (rows, cols), 1)
    row = lax.broadcasted_iota(jnp.int32, (rows, cols), 0)
    lane8 = lax.broadcasted_iota(jnp.int32, (8, cols), 1)
    row8 = lax.broadcasted_iota(jnp.int32, (8, cols), 0)
    ends8 = jnp.logical_or(lane8 == 0, lane8 == cols - 1)
    for q in range(fields):
        vert[q, 0] = jnp.zeros((rows, cols), jnp.float32)
        vert[q, levels + 1] = jnp.zeros((rows, cols), jnp.float32)

    @pl.when(bottom)
    def _():
        south_in[...] = jnp.zeros_like(south_in)
        top_south_in[...] = jnp.zeros_like(top_south_in)

    def remote(step, which, src, dst, peer):
        return pltpu.make_async_remote_copy(
            src_ref=src, dst_ref=dst, send_sem=send_sem.at[step, which],
            recv_sem=recv_sem.at[step, which], device_id=peer, device_id_type=MESH,
        )

    def row_copies(step, which_n, which_s, n_out, s_out, n_in, s_in, part=()):
        at = (step,) + part
        return [
            (remote(step, which_s, n_out.at[at], s_in.at[at], north), jnp.logical_not(top)),
            (remote(step, which_n, n_out.at[at], n_in.at[at], mirror), top),
            (remote(step, which_n, s_out.at[at], n_in.at[at], south), jnp.logical_not(bottom)),
        ]

    def start_rows(copies):
        for copy, go in copies:
            pl.when(go)(copy.start)

    half = fields // 2

    def edges(step, moment, k, src, packed, place, put_rows):
        mask = mask_i[...].astype(jnp.float32)
        d, z = diff[moment, k] * mask, vel[moment, 0, k] * mask
        v = mix[moment, k] * mask
        both = d + jnp.where(lane == cols - 1, -z, z)
        last, first = slice(rows - 1, rows), slice(0, 1)
        b_last, b_first = vel[moment, 1, k, last] * mask[last], vel[moment, 1, k, first] * mask[first]
        to_north, to_south = d[last] - b_last, d[first] + b_first
        packed = list(packed)
        for q in range(fields):
            a = src[q, k]
            vert[q, k + 1] = v * a
            slot, spot = place(q)
            turned = pltpu.roll(both * a, 2 * spot + 1, 1)
            packed[slot] = jnp.where((lane >> 1) == spot, turned, packed[slot])
            put_rows(q, to_north * a[last], to_south * a[first])
        return tuple(packed)

    def interior(moment, k, src, dst):
        mask = mask_i[...].astype(jnp.float32)
        d, z, b = diff[moment, k] * mask, vel[moment, 0, k] * mask, vel[moment, 1, k] * mask
        own = mask - 4.0 * d - 2.0 * (mix[moment, k] * mask)
        eastward = jnp.where(lane == cols - 1, 0.0, d - z)
        westward = jnp.where(lane == 0, 0.0, d + z)
        northward = jnp.where(row == rows - 1, 0.0, d - b)
        southward = jnp.where(row == 0, 0.0, d + b)
        for q in range(fields):
            a = src[q, k]
            total = own * a + vert[q, k] + vert[q, k + 2]
            total = total + pltpu.roll(eastward * a, 1, 1) + pltpu.roll(westward * a, cols - 1, 1)
            total = total + pltpu.roll(northward * a, 1, 0) + pltpu.roll(southward * a, rows - 1, 0)
            dst[q, k] = total

    def finish(k, q, dst, packed, spot, from_south, from_north):
        parts = []
        for r in range(0, rows, 8):
            turned = pltpu.roll(packed[r:r + 8], cols - 1 - 2 * spot, 1)
            total = dst[q, k, r:r + 8] + jnp.where(ends8, turned, 0.0)
            if r == 0:
                total = total + jnp.where(row8 == 0, from_south, 0.0)
            if r == rows - 8:
                total = total + jnp.where(row8 == 7, from_north, 0.0)
            dst[q, k, r:r + 8] = total
            parts.append(total)
        return jnp.concatenate(parts, axis=0)

    def joined(from_west, from_east, turn_west, turn_east):
        if turn_west:
            from_west = pltpu.roll(from_west, turn_west, 1)
        if turn_east:
            from_east = pltpu.roll(from_east, turn_east, 1)
        return jnp.where((lane & 1) == 1, from_west, from_east)

    loads[0].wait()
    zero = jnp.zeros((rows, cols), jnp.float32)
    sums = (zero,) * fields
    for c in range(chunk):
        loads[3 + c].wait()

        def add(k, sums):
            live = k < depth[...]
            return tuple(s + jnp.where(live, field_a[q, k], 0.0) for q, s in enumerate(sums))

        sums = levels_loop(c * span, (c + 1) * span, add, sums, 4)
    loads[1].wait()
    loads[2].wait()

    @pl.when(bottom)
    def _():
        pl.semaphore_wait(barrier, 4)

    @pl.when(jnp.logical_not(bottom))
    def _():
        pl.semaphore_wait(barrier, 5)

    pending = []
    stores = []
    for step in range(steps):
        moment = steps - 1 - step
        src, dst = (field_a, field_b) if step % 2 == 0 else (field_b, field_a)
        final = step == steps - 1
        if final:
            dst = out_h.at[0]
        scale = 1.0 / depth[...].astype(jnp.float32)
        for q in range(fields):
            share[step, q] = weight[q] * (scale * sums[q])
        couple = remote(step, COUPLE, share.at[step], flux.at[step], partner)
        couple.start()
        for copy in coeffs[moment]:
            copy.wait()

        for q in range(fields):
            north_out[step, q, 0:1] = jnp.zeros((1, cols), jnp.float32)
            south_out[step, q, 0:1] = jnp.zeros((1, cols), jnp.float32)

        def deep(k, packed):
            def put(q, up, down):
                north_out[step, q, pl.ds(k, 1)] = up
                south_out[step, q, pl.ds(k, 1)] = down

            return edges(
                step, moment, k, src, packed, lambda q: (q // half, (q % half) * levels + k), put
            )

        packed = (zero, zero)
        groups = []
        for c in range(chunk):
            packed = levels_loop(max(1, c * span), (c + 1) * span, deep, packed, EDGE)
            part = pl.ds(c * span, span)
            which_n, which_s = (ROW_N, ROW_S) if c == 0 else (7 + 2 * c, 8 + 2 * c)
            groups.append(row_copies(
                step, which_n, which_s, north_out, south_out, north_in, south_in, (slice(None), part)
            ))
            start_rows(groups[-1])
        odd = (lane & 1) == 1
        col_out[step, 0] = jnp.where(odd, pltpu.roll(packed[1], 1, 1), packed[0])
        col_out[step, 1] = jnp.where(odd, packed[1], pltpu.roll(packed[0], cols - 1, 1))
        send_e = remote(step, COL_E, col_out.at[step, 0], col_w.at[step], east)
        send_w = remote(step, COL_W, col_out.at[step, 1], col_e.at[step], west)
        send_e.start()
        send_w.start()

        couple.wait_recv()
        for q in range(fields):
            src[q, 0] = src[q, 0] + (flux[step, q] - share[step, q])

        def put_top(q, up, down):
            top_north_out[step, q:q + 1] = up
            top_south_out[step, q:q + 1] = down

        (top_packed,) = edges(step, moment, 0, src, (zero,), lambda q: (0, q), put_top)
        top_col_out[step] = top_packed
        top_e = remote(step, TOP_E, top_col_out.at[step], top_col_w.at[step], east)
        top_w = remote(step, TOP_W, top_col_out.at[step], top_col_e.at[step], west)
        top_rows = row_copies(
            step, TOP_N, TOP_S, top_north_out, top_south_out, top_north_in, top_south_in
        )
        start_rows(top_rows)
        top_e.start()
        top_w.start()

        def inner(k, carry):
            interior(moment, k, src, dst)
            return carry

        levels_loop(0, levels, inner, 0, INNER)

        for copy in (send_e, send_w, top_e, top_w):
            copy.wait_recv()
        for copies in groups + [top_rows]:
            copies[1][0].wait_recv()
            pl.when(jnp.logical_not(bottom))(copies[0][0].wait_recv)

        @pl.when(top)
        def _():
            lane_s = lax.broadcasted_iota(jnp.int32, (levels, cols), 1)
            for q in range(fields):
                turned = reversed_lanes(north_in[step, q], lane_s)
                north_in[step, q] = turned if q < half else -turned
            lane_f = lax.broadcasted_iota(jnp.int32, (fields, cols), 1)
            sign = lax.broadcasted_iota(jnp.int32, (fields, cols), 0)
            turned = reversed_lanes(top_north_in[step], lane_f)
            top_north_in[step] = jnp.where(sign < half, turned, -turned)

        pair = [
            joined(col_w[step], col_e[step], 1, 0), joined(col_w[step], col_e[step], 0, cols - 1)
        ]
        top_pair = joined(top_col_w[step], top_col_e[step], 1, cols - 1)
        sums = []
        for q in range(fields):
            total = finish(
                0, q, dst, top_pair, q,
                top_south_in[step, q:q + 1], top_north_in[step, q:q + 1],
            )
            sums.append(total)
        sums = tuple(sums)
        for c in range(chunk):

            def last(k, sums):
                out = []
                for q in range(fields):
                    total = finish(
                        k, q, dst, pair[q // half], (q % half) * levels + k,
                        south_in[step, q, pl.ds(k, 1)], north_in[step, q, pl.ds(k, 1)],
                    )
                    if not final:
                        out.append(sums[q] + jnp.where(k < depth[...], total, 0.0))
                return tuple(out) if not final else sums

            lower = max(1, c * span)
            sums = levels_loop(lower, (c + 1) * span, last, sums if not final else 0, LAST)

        pending += [(couple, None), (send_e, None), (send_w, None), (top_e, None), (top_w, None)]
        for copies in groups + [top_rows]:
            pending += copies

    for copy, go in pending:
        if go is None:
            copy.wait_send()
        else:
            pl.when(go)(copy.wait_send)
    for copy in stores:
        copy.wait()


def solution(mesh):
    lats, lons = mesh.shape["lat"], mesh.shape["lon"]

    def shards(adjoint, land_mask, coupling_depth, coupling_weight, diffusion, velocity, mixing):
        _, fields, levels, rows, cols = adjoint.shape
        steps = diffusion.shape[0]
        chunk = 3
        f32 = jnp.float32
        block = (rows, cols)
        column = pltpu.VMEM((steps, 2, rows, cols), f32)
        top_column = pltpu.VMEM((steps, rows, cols), f32)
        edge = pltpu.VMEM((steps, fields, levels, cols), f32)
        top_edge = pltpu.VMEM((steps, fields, cols), f32)
        return pl.pallas_call(
            functools.partial(kernel, lats, lons),
            out_shape=jax.ShapeDtypeStruct(adjoint.shape, f32),
            in_specs=[pl.BlockSpec(memory_space=pltpu.HBM)] * 7,
            out_specs=pl.BlockSpec(memory_space=pltpu.VMEM),
            scratch_shapes=[
                pltpu.VMEM((fields, levels, rows, cols), f32),
                pltpu.VMEM((fields, levels, rows, cols), f32),
                pltpu.VMEM((steps, levels, rows, cols), f32),
                pltpu.VMEM((steps, 2, levels, rows, cols), f32),
                pltpu.VMEM((steps, levels, rows, cols), f32),
                pltpu.VMEM(block, jnp.int32),
                pltpu.VMEM(block, jnp.int32),
                pltpu.VMEM((fields, rows, cols), f32),
                pltpu.VMEM((fields, levels + 2, rows, cols), f32),
                pltpu.VMEM((steps, fields, rows, cols), f32),
                pltpu.VMEM((steps, fields, rows, cols), f32),
                column, top_column, top_column,
                top_column, top_column, top_column,
                edge, edge, edge, edge,
                top_edge, top_edge, top_edge, top_edge,
                pltpu.SemaphoreType.DMA((3 + chunk + 3 * steps,)),
                pltpu.SemaphoreType.DMA((chunk,)),
                pltpu.SemaphoreType.DMA((steps, 7 + 2 * chunk)),
                pltpu.SemaphoreType.DMA((steps, 7 + 2 * chunk)),
            ],
            compiler_params=pltpu.CompilerParams(
                collective_id=0, has_side_effects=True, vmem_limit_bytes=40 * 1024 * 1024
            ),
            name="adjoint",
        )(*(pltpu.with_memory_space_constraint(x, pltpu.HBM) for x in (adjoint, land_mask, coupling_depth, coupling_weight, diffusion, velocity, mixing)))

    in_specs = (
        P("ice", None, None, "lat", "lon"),
        P("lat", "lon"),
        P("ice", "lat", "lon"),
        P("ice", None, "lat", "lon"),
        P(None, "ice", None, "lat", "lon"),
        P(None, "ice", None, None, "lat", "lon"),
        P(None, "ice", None, "lat", "lon"),
    )
    out_specs = P("ice", None, None, "lat", "lon")
    return jax.shard_map(shards, mesh=mesh, in_specs=in_specs, out_specs=out_specs, check_vma=False)
```

```python
import functools

import jax
import jax.numpy as jnp
from jax import lax
from jax.experimental import pallas as pl
from jax.experimental.pallas import tpu as pltpu
from jax.sharding import PartitionSpec as P

MESH = pl.DeviceIdType.MESH
INNER, SUM, PIECES = 7, 4, 2
COUPLE, COL_E, COL_W, ROW_N, ROW_S, SIDE_E, SIDE_W, SIDE_N, SIDE_S, CROSS_E, CROSS_W, CROSS_N, CROSS_S = range(13)
COPIES = 13
EAST, WEST, NORTH, SOUTH = 0, 1, 0, 1


def levels_loop(lower, upper, body, carry, times):
    whole = (upper - lower) // times

    def some(i, carry):
        for j in range(times):
            carry = body(lower + i * times + j, carry)
        return carry

    if whole > 0:
        carry = lax.fori_loop(0, whole, some, carry)
    for k in range(lower + whole * times, upper):
        carry = body(k, carry)
    return carry


def finished(value, pair, row_got, spot, slot):
    rows, cols = value.shape
    lane8 = lax.broadcasted_iota(jnp.int32, (8, cols), 1)
    row8 = lax.broadcasted_iota(jnp.int32, (8, cols), 0)
    ends8 = jnp.logical_or(lane8 == 0, lane8 == cols - 1)
    parts = []
    for r in range(0, rows, 8):
        turned = pltpu.roll(pair[r:r + 8], cols - 1 - 2 * spot, 1)
        total = value[r:r + 8] + jnp.where(ends8, turned, 0.0)
        if r == 0:
            total = total + jnp.where(row8 == 0, row_got[SOUTH, slot:slot + 1], 0.0)
        if r == rows - 8:
            total = total + jnp.where(row8 == 7, row_got[NORTH, slot:slot + 1], 0.0)
        parts.append(total)
    return jnp.concatenate(parts, axis=0)


def finish_kernel(value, pair, row_got, out_h, done, sems):
    _, fields, levels, rows, cols = value.shape
    half = fields // 2
    pairs = [pair[i] for i in range(half)]
    pieces = sems.shape[0] // fields
    span = levels // pieces
    copies = []
    for q in range(fields):
        for k in range(levels):
            slot = 2 * levels * (q % half) + 2 * k + q // half
            done[q, k] = finished(value[0, q, k], pairs[q // half], row_got, (q % half) * levels + k, slot)
            if (k + 1) % span == 0:
                part = pl.ds(k + 1 - span, span)
                copies.append(pltpu.make_async_copy(done.at[q, part], out_h.at[0, q, part], sems.at[len(copies)]))
                copies[-1].start()
    for copy in copies:
        copy.wait()


def kernel(
    lats, lons, adj_h, mask_h, depth_h, weight_h, diff_h, vel_h, mix_h,
    out_v, pair_v, row_got,
    field_a, field_b, diff, vel, mix, mask_i, depth, weight, mask_f,
    share, flux, col_depth, col_rate, col_coef, row_rate, row_coef, row_own,
    col_out, col_in, col_side_out, col_side_in, row_out, row_in, row_side_out, row_side_in,
    load_sem, send_sem, recv_sem,
):
    fields, levels, rows, cols = field_a.shape
    steps = diff.shape[0]
    half = fields // 2
    group = 2 * levels
    slots = fields * levels
    ice, lat, lon = lax.axis_index("ice"), lax.axis_index("lat"), lax.axis_index("lon")
    top, bottom = lat == lats - 1, lat == 0
    lon_e, lon_w = lax.rem(lon + 1, lons), lax.rem(lon + lons - 1, lons)
    lat_n = jnp.where(top, lat, lat + 1)
    lon_n = jnp.where(top, lons - 1 - lon, lon)
    lat_s = jnp.where(bottom, 0, lat - 1)
    partner = (1 - ice, lat, lon)
    east, west, north, south = [
        [(section, y, x) for section in (ice, 1 - ice)]
        for y, x in ((lat, lon_e), (lat, lon_w), (lat_n, lon_n), (lat_s, lon))
    ]

    first = [
        pltpu.make_async_copy(depth_h.at[0], depth, load_sem.at[0]),
        pltpu.make_async_copy(weight_h.at[0], weight, load_sem.at[1]),
        pltpu.make_async_copy(mask_h, mask_i, load_sem.at[2]),
    ]
    coeffs = []
    for moment in range(steps - 1):
        base = 12 + 3 * moment
        coeffs.append([
            pltpu.make_async_copy(diff_h.at[moment, 0], diff.at[moment], load_sem.at[base]),
            pltpu.make_async_copy(vel_h.at[moment, 0], vel.at[moment], load_sem.at[base + 1]),
            pltpu.make_async_copy(mix_h.at[moment, 0], mix.at[moment], load_sem.at[base + 2]),
        ])
    moment = steps - 1
    last_mix = pltpu.make_async_copy(mix_h.at[moment, 0], mix.at[moment], load_sem.at[12 + 3 * moment])
    parts = []
    for i, (r, n) in enumerate(((rows - 8, 8), (0, 8), (8, rows - 16))):
        part = pl.ds(r, n)
        parts.append([
            pltpu.make_async_copy(adj_h.at[0, :, :, part], field_a.at[:, :, part], load_sem.at[3 + i]),
            pltpu.make_async_copy(diff_h.at[moment, 0, :, part], diff.at[moment, :, part], load_sem.at[6 + i]),
            pltpu.make_async_copy(vel_h.at[moment, 0, :, :, part], vel.at[moment, :, :, part], load_sem.at[9 + i]),
        ])
    for copies in [first] + parts + [[last_mix]] + coeffs[::-1]:
        for copy in copies:
            copy.start()

    barrier = pltpu.get_barrier_semaphore()
    for peer in [partner] + east + west + north:
        pl.semaphore_signal(barrier, inc=1, device_id=peer, device_id_type=MESH)

    @pl.when(jnp.logical_not(bottom))
    def _():
        for peer in south:
            pl.semaphore_signal(barrier, inc=1, device_id=peer, device_id_type=MESH)

    lane = lax.broadcasted_iota(jnp.int32, (rows, cols), 1)
    row = lax.broadcasted_iota(jnp.int32, (rows, cols), 0)
    odd = (lane & 1) == 1
    low = lane < group
    used = lane < slots
    lane_level = jnp.where(low, lane, lane - group) >> 1
    lane8 = lax.broadcasted_iota(jnp.int32, (8, cols), 1)
    row8 = lax.broadcasted_iota(jnp.int32, (8, cols), 0)
    ends8 = jnp.logical_or(lane8 == 0, lane8 == cols - 1)
    slot_row = lax.broadcasted_iota(jnp.int32, (slots, cols), 0)
    slot_lane = lax.broadcasted_iota(jnp.int32, (slots, cols), 1)
    slot_level = jnp.where(slot_row < group, slot_row, slot_row - group) >> 1
    zero = jnp.zeros((rows, cols), jnp.float32)
    f32 = jnp.float32

    def slot_of(q, k):
        return group * (q % half) + 2 * k + q // half

    @pl.when(bottom)
    def _():
        row_in[:, SOUTH] = jnp.zeros_like(row_in[:, SOUTH])
        row_side_in[:, :, SOUTH] = jnp.zeros_like(row_side_in[:, :, SOUTH])

    def remote(step, which, src, dst, peer):
        return pltpu.make_async_remote_copy(
            src_ref=src, dst_ref=dst, send_sem=send_sem.at[step, which],
            recv_sem=recv_sem.at[step, which], device_id=peer, device_id_type=MESH,
        )

    def col_copies(step):
        return [
            (remote(step, COL_E, col_out.at[step, EAST], col_in.at[step, WEST], east[0]), None),
            (remote(step, COL_W, col_out.at[step, WEST], col_in.at[step, EAST], west[0]), None),
        ]

    def row_pair(step, which_n, which_s, out, into, section):
        north_in, south_in = into(NORTH), into(SOUTH)
        peer_n, peer_s = north[section], south[section]
        return [
            (remote(step, which_n, out.at[step, NORTH], north_in, peer_n), top),
            (remote(step, which_s, out.at[step, NORTH], south_in, peer_n), jnp.logical_not(top)),
            (remote(step, which_n, out.at[step, SOUTH], north_in, peer_s), jnp.logical_not(bottom)),
        ]

    def row_copies(step):
        return row_pair(step, ROW_N, ROW_S, row_out, lambda side: row_in.at[step, side], 0)

    def side_copies(step):
        copies = []
        for section, names in enumerate(((SIDE_E, SIDE_W, SIDE_N, SIDE_S), (CROSS_E, CROSS_W, CROSS_N, CROSS_S))):
            for which, side, peer in ((names[0], EAST, east), (names[1], WEST, west)):
                copies.append((remote(
                    step, which, col_side_out.at[step, side], col_side_in.at[step, section, 1 - side], peer[section]
                ), None))
            copies += row_pair(
                step, names[2], names[3], row_side_out, lambda side: row_side_in.at[step, section, side], section
            )
        return copies

    def start(copies):
        for copy, go in copies:
            if go is None:
                copy.start()
            else:
                pl.when(go)(copy.start)

    def start_rows(copies):
        odd_lat = lax.rem(lat, 2) == 1
        even_lat = jnp.logical_not(odd_lat)
        start([(copy, jnp.logical_and(go, odd_lat)) for copy, go in copies[:2]])
        start(copies[2:])
        start([(copy, jnp.logical_and(go, even_lat)) for copy, go in copies[:2]])

    def wait_recv(copies):
        rest = []
        for copy, go in copies:
            if go is None:
                copy.wait_recv()
            else:
                rest.append(copy)
        for i in range(0, len(rest), 3):
            rest[i].wait_recv()
            pl.when(jnp.logical_not(bottom))(rest[i + 1].wait_recv)

    def pack(packed, q, k, value):
        slot, spot = q // half, (q % half) * levels + k
        turned = pltpu.roll(value, 2 * spot + 1, 1)
        packed = list(packed)
        packed[slot] = jnp.where((lane >> 1) == spot, turned, packed[slot])
        return tuple(packed)

    def gather(packed, src, lower, upper):
        for k in range(lower, upper):
            for q in range(fields):
                packed = pack(packed, q, k, src[q, k])
        return packed

    def split(packed):
        east_side = jnp.where(odd, pltpu.roll(packed[1], 1, 1), packed[0])
        west_side = jnp.where(odd, packed[1], pltpu.roll(packed[0], cols - 1, 1))
        return east_side, west_side

    def joined(from_west, from_east):
        first = jnp.where(odd, pltpu.roll(from_west, 1, 1), from_east)
        second = jnp.where(odd, from_west, pltpu.roll(from_east, cols - 1, 1))
        return first, second

    def take_row(src, side):
        flat = src.reshape(fields, levels * rows, cols)
        r = (rows - 1, 0)[side]
        for q in range(fields):
            row_own[side, pl.ds(slot_of(q, 0), levels, stride=2)] = flat[q, pl.ds(r, levels, stride=rows)]

    def row_coefs(moment, side):
        diff_rows, vel_rows = diff.reshape(steps, levels * rows, cols), vel.reshape(steps, 2, levels * rows, cols)
        r, sign = ((rows - 1, -1.0), (0, 1.0))[side]
        line = pl.ds(r, levels, stride=rows)
        value = (diff_rows[moment, line] + sign * vel_rows[moment, 1, line]) * mask_f[r:r + 1]
        for g in range(half):
            for p in range(2):
                row_coef[moment * 2 + side, pl.ds(g * group + p, levels, stride=2)] = value

    def col_coefs(moment):
        packed = zero
        for k in range(levels):
            d, z = diff[moment, k] * mask_f[...], vel[moment, 0, k] * mask_f[...]
            both = d + jnp.where(lane == cols - 1, -z, z)
            turned = pltpu.roll(both, 2 * k + 1, 1)
            packed = jnp.where((lane >> 1) == k, turned, packed)
        for side, value in (
            (EAST, jnp.where(odd, pltpu.roll(packed, 1, 1), packed)),
            (WEST, jnp.where(odd, packed, pltpu.roll(packed, cols - 1, 1))),
        ):
            col_coef[moment, side] = jnp.where(low, value, pltpu.roll(value, group, 1))

    def edge_rates():
        inverse = 1.0 / depth[...].astype(f32)
        for side, c in ((EAST, cols - 1), (WEST, 0)):
            rate = zero
            for q in range(fields):
                own = jnp.broadcast_to((weight[q] * inverse)[:, c:c + 1], (rows, cols))
                rate = jnp.where(lane == slot_of(q, 0), own, rate)
            col_rate[side] = rate
            col_depth[side] = jnp.broadcast_to(depth[:, c:c + 1], (rows, cols))
        for side, r in ((NORTH, rows - 1), (SOUTH, 0)):
            for g in range(half):
                rate = jnp.zeros((8, cols), f32)
                for p in range(2):
                    own = weight[g + p * half, r:r + 1] * inverse[r:r + 1]
                    rate = jnp.where(row8 == p, own, rate)
                row_rate[side, g] = rate

    def put_cols(step, moment, sides):
        for side, value in zip((EAST, WEST), sides):
            coef = col_coef[moment, side]
            col_out[step, side] = jnp.where(used, coef * value, pltpu.roll(coef, slots, 1))

    def put_row(step, moment, side, value):
        row_out[step, side, 0:slots] = row_coef[moment * 2 + side] * value
        row_out[step, side, slots:slots + 8] = row_coef[moment * 2 + side, 0:8]

    def put_sides(step, col_sides, row_sides):
        for side, value in zip((EAST, WEST), col_sides):
            total = jnp.where(jnp.logical_and(used, lane_level < col_depth[side]), value, 0.0)
            turns = [pltpu.roll(total, cols - n, 1) for n in (2, 4, 6)]
            total = (total + turns[0]) + (turns[1] + turns[2])
            turns = [pltpu.roll(total, cols - n, 1) for n in (8, 16, 24, 32, 40)]
            total = ((total + turns[0]) + (turns[1] + turns[2])) + (turns[3] + turns[4])
            given = col_rate[side] * total
            out = given[0:8]
            for i in range(1, rows // 8):
                out = out + pltpu.roll(given[8 * i:8 * i + 8], 2 * i, 1)
            col_side_out[step, side] = out
        for side, value, r in zip((NORTH, SOUTH), row_sides, (rows - 1, 0)):
            live = jnp.where(slot_level < depth[r:r + 1], value, 0.0)
            out = jnp.zeros((8, cols), f32)
            for g in range(half):
                total = live[g * group:g * group + 8]
                for i in range(8, group, 8):
                    total = total + live[g * group + i:g * group + i + 8]
                total = (total + pltpu.roll(total, 2, 0)) + (pltpu.roll(total, 4, 0) + pltpu.roll(total, 6, 0))
                given = row_rate[side, g] * total
                out = out + (pltpu.roll(given, 2 * g, 0) if g else given)
            row_side_out[step, side] = out

    def receive(step):
        got = []
        for side in (EAST, WEST):
            value = col_in[step, side]
            coef = jnp.where(low, pltpu.roll(value, cols - slots, 1), pltpu.roll(value, cols - slots + group, 1))
            given = col_side_in[step, 1, side] - col_side_in[step, 0, side]
            given = jnp.concatenate(
                [given] + [pltpu.roll(given, cols - 2 * i, 1) for i in range(1, rows // 8)], axis=0
            )
            term = jnp.where(lane_level == 0, coef * given, 0.0)
            got.append(jnp.where(used, value + term, 0.0))
        for side in (NORTH, SOUTH):
            given = row_side_in[step, 1, side] - row_side_in[step, 0, side]
            coef = row_in[step, side, slots:slots + 1]
            for g in range(half):
                block = slice(g * group, g * group + 8)
                term = pltpu.roll(given, 8 - 2 * g, 0) if g else given
                term = jnp.where(row8 < 2, coef * term, 0.0)
                row_got[side, block] = row_in[step, side, block] + term
                block = slice(g * group + 8, (g + 1) * group)
                row_got[side, block] = row_in[step, side, block]

        @pl.when(top)
        def _():
            value = row_got[NORTH]
            turned = jnp.take_along_axis(value, cols - 1 - slot_lane, axis=1)
            row_got[NORTH] = jnp.where((slot_row & 1) == 1, -turned, turned)

        return got

    def col_corner(side):
        value, out = row_got[side], []
        for c in (cols - 1, 0):
            whole = jnp.broadcast_to(value[:, c:c + 1], (slots, cols))
            whole = jnp.where(slot_lane == slot_row, whole, 0.0)
            out.append(jnp.sum(whole, axis=0, keepdims=True))
        return out

    def row_corners(got_e, got_w):
        ends = jnp.where(row8 == 0, got_e[rows - 1:rows], 0.0)
        for i, line in ((1, got_w[rows - 1:rows]), (2, got_e[0:1]), (3, got_w[0:1])):
            ends = jnp.where(row8 == i, line, ends)
        high = ends.astype(jnp.bfloat16)
        ends = ends - high.astype(f32)
        middle = ends.astype(jnp.bfloat16)
        small = (ends - middle.astype(f32)).astype(jnp.bfloat16)
        three = jnp.concatenate([x.astype(f32) for x in (high, middle, small)], axis=0).astype(jnp.bfloat16)
        lane_p = lax.broadcasted_iota(jnp.int32, (24, 2 * cols), 1)
        row_p = lax.broadcasted_iota(jnp.int32, (24, 2 * cols), 0) & 7
        pick = jnp.where(row_p == 0, cols - 1, jnp.where(row_p == 1, 0, jnp.where(row_p == 2, 2 * cols - 1, cols)))
        pick = jnp.where(jnp.logical_and(row_p < 4, lane_p == pick), 1.0, 0.0).astype(jnp.bfloat16)
        both = lax.dot_general(three, pick, (((0,), (0,)), ((), ())), preferred_element_type=f32)
        return both[0:slots, 0:cols], both[0:slots, cols:2 * cols]

    def interior(moment, k, src, dst, first=False, last=False):
        mask = mask_f[...]
        d, z, b = diff[moment, k] * mask, vel[moment, 0, k] * mask, vel[moment, 1, k] * mask
        own = mask - 4.0 * d - 2.0 * (mix[moment, k] * mask)
        above = None if first else mix[moment, k - 1] * mask
        below = None if last else mix[moment, k + 1] * mask
        eastward = jnp.where(lane == cols - 1, 0.0, d - z)
        westward = jnp.where(lane == 0, 0.0, d + z)
        northward = jnp.where(row == rows - 1, 0.0, d - b)
        southward = jnp.where(row == 0, 0.0, d + b)
        for q in range(fields):
            a = src[q, k]
            total = own * a
            if not first:
                total = total + above * src[q, k - 1]
            if not last:
                total = total + below * src[q, k + 1]
            total = total + pltpu.roll(eastward * a, 1, 1) + pltpu.roll(westward * a, cols - 1, 1)
            total = total + pltpu.roll(northward * a, 1, 0) + pltpu.roll(southward * a, rows - 1, 0)
            dst[q, k] = total

    for copy in first:
        copy.wait()
    mask_f[...] = mask_i[...].astype(f32)
    edge_rates()
    for side in (NORTH, SOUTH):
        for copy in parts[side]:
            copy.wait()
        take_row(field_a, side)
        row_coefs(steps - 1, side)
        put_row(0, steps - 1, side, row_own[side])

    @pl.when(bottom)
    def _():
        pl.semaphore_wait(barrier, 7)

    @pl.when(jnp.logical_not(bottom))
    def _():
        pl.semaphore_wait(barrier, 9)

    row_halo = row_copies(0)
    start_rows(row_halo)
    for copy in parts[2]:
        copy.wait()
    own_cols = split(gather((zero, zero), field_a, 0, levels))
    col_coefs(steps - 1)
    put_cols(0, steps - 1, own_cols)
    col_halo = col_copies(0)
    start(col_halo)
    put_sides(0, own_cols, (row_own[NORTH], row_own[SOUTH]))
    side_halo = side_copies(0)
    start(side_halo)
    halo = row_halo + col_halo + side_halo
    pending = halo

    def add(k, sums):
        live = k < depth[...]
        return tuple(s + jnp.where(live, field_a[q, k], 0.0) for q, s in enumerate(sums))

    sums = levels_loop(0, levels, add, (zero,) * fields, SUM)
    last_mix.wait()

    for step in range(steps):
        moment = steps - 1 - step
        src, dst = (field_a, field_b) if step % 2 == 0 else (field_b, field_a)
        final = step == steps - 1
        if final:
            dst = out_v.at[0]
        scale = 1.0 / depth[...].astype(f32)
        for q in range(fields):
            share[step, q] = weight[q] * (scale * sums[q])
        couple = remote(step, COUPLE, share.at[step], flux.at[step], partner)
        couple.start()
        pending = pending + [(couple, None)]

        def inner(k, carry, **ends):
            interior(moment, k, src, dst, **ends)
            return carry

        levels_loop(2, levels - 1, inner, 0, INNER)
        inner(levels - 1, 0, last=True)
        couple.wait_recv()
        for q in range(fields):
            src[q, 0] = src[q, 0] + (flux[step, q] - share[step, q])
        inner(0, 0, first=True)
        inner(1, 0)
        if not final:
            own_e, own_w = split(gather((zero, zero), dst, 0, levels))
            for copy in coeffs[moment - 1]:
                copy.wait()
            for side in (NORTH, SOUTH):
                take_row(dst, side)
                row_coefs(moment - 1, side)
            col_coefs(moment - 1)

        wait_recv(halo)
        got_e, got_w = receive(step)
        if not final:
            row_more = row_corners(got_e, got_w)
            row_sides = []
            for side in (NORTH, SOUTH):
                row_sides.append(row_own[side] + row_got[side] + row_more[side])
                put_row(step + 1, moment - 1, side, row_sides[side])
            row_halo = row_copies(step + 1)
            start_rows(row_halo)
            col_more = col_corner(NORTH), col_corner(SOUTH)
            col_sides = []
            for side, value in ((EAST, own_e + got_e), (WEST, own_w + got_w)):
                value = value + jnp.where(row == rows - 1, col_more[NORTH][side], 0.0)
                col_sides.append(value + jnp.where(row == 0, col_more[SOUTH][side], 0.0))
            put_cols(step + 1, moment - 1, col_sides)
            col_halo = col_copies(step + 1)
            start(col_halo)
            put_sides(step + 1, col_sides, row_sides)
            side_halo = side_copies(step + 1)
            start(side_halo)
            halo = row_halo + col_halo + side_halo
            pending = pending + halo

        pair = joined(got_w, got_e)
        if final:
            pair_v[0], pair_v[1] = pair
            break

        sums = [zero] * fields
        for k in range(levels):
            for q in range(fields):
                total = finished(dst[q, k], pair[q // half], row_got, (q % half) * levels + k, slot_of(q, k))
                dst[q, k] = total
                sums[q] = sums[q] + jnp.where(k < depth[...], total, 0.0)

    for copy, go in pending:
        if go is None:
            copy.wait_send()
        else:
            pl.when(go)(copy.wait_send)


def solution(mesh):
    lats, lons = mesh.shape["lat"], mesh.shape["lon"]

    def shards(adjoint, land_mask, coupling_depth, coupling_weight, diffusion, velocity, mixing):
        _, fields, levels, rows, cols = adjoint.shape
        steps = diffusion.shape[0]
        f32 = jnp.float32
        block = (rows, cols)
        slots = fields * levels
        column = pltpu.VMEM((steps, 2, rows, cols), f32)
        edge = pltpu.VMEM((steps, 2, slots + 8, cols), f32)
        side_out, side_in = pltpu.VMEM((steps, 2, 8, cols), f32), pltpu.VMEM((steps, 2, 2, 8, cols), f32)
        parts = pl.pallas_call(
            functools.partial(kernel, lats, lons),
            out_shape=(
                jax.ShapeDtypeStruct(adjoint.shape, f32),
                jax.ShapeDtypeStruct((2, rows, cols), f32),
                jax.ShapeDtypeStruct((2, slots, cols), f32),
            ),
            in_specs=[pl.BlockSpec(memory_space=pltpu.HBM)] * 7,
            out_specs=(pl.BlockSpec(memory_space=pltpu.VMEM),) * 3,
            scratch_shapes=[
                pltpu.VMEM((fields, levels, rows, cols), f32),
                pltpu.VMEM((fields, levels, rows, cols), f32),
                pltpu.VMEM((steps, levels, rows, cols), f32),
                pltpu.VMEM((steps, 2, levels, rows, cols), f32),
                pltpu.VMEM((steps, levels, rows, cols), f32),
                pltpu.VMEM(block, jnp.int32),
                pltpu.VMEM(block, jnp.int32),
                pltpu.VMEM((fields, rows, cols), f32),
                pltpu.VMEM(block, f32),
                pltpu.VMEM((steps, fields, rows, cols), f32),
                pltpu.VMEM((steps, fields, rows, cols), f32),
                pltpu.VMEM((2, rows, cols), jnp.int32),
                pltpu.VMEM((2, rows, cols), f32),
                column,
                pltpu.VMEM((2, fields // 2, 8, cols), f32),
                pltpu.VMEM((steps * 2, slots, cols), f32),
                pltpu.VMEM((2, slots, cols), f32),
                column, column, side_out, side_in,
                edge, edge, side_out, side_in,
                pltpu.SemaphoreType.DMA((10 + 3 * steps,)),
                pltpu.SemaphoreType.DMA((steps, COPIES)),
                pltpu.SemaphoreType.DMA((steps, COPIES)),
            ],
            compiler_params=pltpu.CompilerParams(
                collective_id=0, has_side_effects=True, vmem_limit_bytes=40 * 1024 * 1024
            ),
            name="adjoint",
        )(*(pltpu.with_memory_space_constraint(x, pltpu.HBM) for x in (adjoint, land_mask, coupling_depth, coupling_weight, diffusion, velocity, mixing)))
        return pl.pallas_call(
            finish_kernel,
            out_shape=jax.ShapeDtypeStruct(adjoint.shape, f32),
            in_specs=[pl.BlockSpec(memory_space=pltpu.VMEM)] * 3,
            out_specs=pl.BlockSpec(memory_space=pltpu.HBM),
            scratch_shapes=[
                pltpu.VMEM((fields, levels, rows, cols), f32), pltpu.SemaphoreType.DMA((PIECES * fields,)),
            ],
            compiler_params=pltpu.CompilerParams(vmem_limit_bytes=16 * 1024 * 1024),
            name="adjoint_finish",
        )(*parts)

    in_specs = (
        P("ice", None, None, "lat", "lon"),
        P("lat", "lon"),
        P("ice", "lat", "lon"),
        P("ice", None, "lat", "lon"),
        P(None, "ice", None, "lat", "lon"),
        P(None, "ice", None, None, "lat", "lon"),
        P(None, "ice", None, "lat", "lon"),
    )
    out_specs = P("ice", None, None, "lat", "lon")
    return jax.shard_map(shards, mesh=mesh, in_specs=in_specs, out_specs=out_specs, check_vma=False)
```

```python
import functools

import jax
import jax.numpy as jnp
from jax import lax
from jax.experimental import pallas as pl
from jax.experimental.pallas import tpu as pltpu
from jax.sharding import PartitionSpec as P

MESH = pl.DeviceIdType.MESH
INNER, SUM, PIECES = 7, 4, 2
COUPLE, COL_E, COL_W, ROW_N, ROW_S, SIDE_E, SIDE_W, SIDE_N, SIDE_S, CROSS_E, CROSS_W, CROSS_N, CROSS_S, EARLY_N, EARLY_S = range(15)
COPIES = 15
EAST, WEST, NORTH, SOUTH = 0, 1, 0, 1


def levels_loop(lower, upper, body, carry, times):
    whole = (upper - lower) // times

    def some(i, carry):
        for j in range(times):
            carry = body(lower + i * times + j, carry)
        return carry

    if whole > 0:
        carry = lax.fori_loop(0, whole, some, carry)
    for k in range(lower + whole * times, upper):
        carry = body(k, carry)
    return carry


def finished(value, pair, row_got, spot, slot):
    rows, cols = value.shape
    lane8 = lax.broadcasted_iota(jnp.int32, (8, cols), 1)
    row8 = lax.broadcasted_iota(jnp.int32, (8, cols), 0)
    ends8 = jnp.logical_or(lane8 == 0, lane8 == cols - 1)
    parts = []
    for r in range(0, rows, 8):
        turned = pltpu.roll(pair[r:r + 8], cols - 1 - 2 * spot, 1)
        total = value[r:r + 8] + jnp.where(ends8, turned, 0.0)
        if r == 0:
            total = total + jnp.where(row8 == 0, row_got[SOUTH, slot:slot + 1], 0.0)
        if r == rows - 8:
            total = total + jnp.where(row8 == 7, row_got[NORTH, slot:slot + 1], 0.0)
        parts.append(total)
    return jnp.concatenate(parts, axis=0)


def finish_kernel(value, pair, row_got, out_h, done, sems):
    _, fields, levels, rows, cols = value.shape
    half = fields // 2
    pairs = [pair[i] for i in range(half)]
    pieces = sems.shape[0] // fields
    span = levels // pieces
    copies = []
    for q in range(fields):
        for k in range(levels):
            slot = 2 * levels * (q % half) + 2 * k + q // half
            done[q, k] = finished(value[0, q, k], pairs[q // half], row_got, (q % half) * levels + k, slot)
            if (k + 1) % span == 0:
                part = pl.ds(k + 1 - span, span)
                copies.append(pltpu.make_async_copy(done.at[q, part], out_h.at[0, q, part], sems.at[len(copies)]))
                copies[-1].start()
    for copy in copies:
        copy.wait()


def kernel(
    lats, lons, adj_h, mask_h, depth_h, weight_h, diff_h, vel_h, mix_h,
    out_v, pair_v, row_got,
    field_a, field_b, diff, vel, mix, mask_i, depth, weight, mask_f,
    share, flux, col_depth, col_rate, col_coef, row_rate, row_coef, row_own, row_keep, row_corner, early_out, early_in,
    col_out, col_in, col_side_out, col_side_in, row_out, row_in, row_side_out, row_side_in,
    load_sem, send_sem, recv_sem,
):
    fields, levels, rows, cols = field_a.shape
    steps = diff.shape[0]
    half = fields // 2
    group = 2 * levels
    slots = fields * levels
    ice, lat, lon = lax.axis_index("ice"), lax.axis_index("lat"), lax.axis_index("lon")
    top, bottom = lat == lats - 1, lat == 0
    lon_e, lon_w = lax.rem(lon + 1, lons), lax.rem(lon + lons - 1, lons)
    lat_n = jnp.where(top, lat, lat + 1)
    lon_n = jnp.where(top, lons - 1 - lon, lon)
    lat_s = jnp.where(bottom, 0, lat - 1)
    partner = (1 - ice, lat, lon)
    east, west, north, south = [
        [(section, y, x) for section in (ice, 1 - ice)]
        for y, x in ((lat, lon_e), (lat, lon_w), (lat_n, lon_n), (lat_s, lon))
    ]

    first = [
        pltpu.make_async_copy(depth_h.at[0], depth, load_sem.at[0]),
        pltpu.make_async_copy(weight_h.at[0], weight, load_sem.at[1]),
        pltpu.make_async_copy(mask_h, mask_i, load_sem.at[2]),
    ]
    coeffs = []
    for moment in range(steps - 1):
        base = 12 + 3 * moment
        coeffs.append([
            pltpu.make_async_copy(diff_h.at[moment, 0], diff.at[moment], load_sem.at[base]),
            pltpu.make_async_copy(vel_h.at[moment, 0], vel.at[moment], load_sem.at[base + 1]),
            pltpu.make_async_copy(mix_h.at[moment, 0], mix.at[moment], load_sem.at[base + 2]),
        ])
    moment = steps - 1
    last_mix = pltpu.make_async_copy(mix_h.at[moment, 0], mix.at[moment], load_sem.at[12 + 3 * moment])
    parts = []
    for i, (r, n) in enumerate(((rows - 8, 8), (0, 8), (8, rows - 16))):
        part = pl.ds(r, n)
        parts.append([
            pltpu.make_async_copy(adj_h.at[0, :, :, part], field_a.at[:, :, part], load_sem.at[3 + i]),
            pltpu.make_async_copy(diff_h.at[moment, 0, :, part], diff.at[moment, :, part], load_sem.at[6 + i]),
            pltpu.make_async_copy(vel_h.at[moment, 0, :, :, part], vel.at[moment, :, :, part], load_sem.at[9 + i]),
        ])
    for copies in [first] + parts + [[last_mix]] + coeffs[::-1]:
        for copy in copies:
            copy.start()

    barrier = pltpu.get_barrier_semaphore()
    for peer in [partner] + east + west + north:
        pl.semaphore_signal(barrier, inc=1, device_id=peer, device_id_type=MESH)

    @pl.when(jnp.logical_not(bottom))
    def _():
        for peer in south:
            pl.semaphore_signal(barrier, inc=1, device_id=peer, device_id_type=MESH)

    lane = lax.broadcasted_iota(jnp.int32, (rows, cols), 1)
    row = lax.broadcasted_iota(jnp.int32, (rows, cols), 0)
    odd = (lane & 1) == 1
    low = lane < group
    used = lane < slots
    lane_level = jnp.where(low, lane, lane - group) >> 1
    lane8 = lax.broadcasted_iota(jnp.int32, (8, cols), 1)
    row8 = lax.broadcasted_iota(jnp.int32, (8, cols), 0)
    ends8 = jnp.logical_or(lane8 == 0, lane8 == cols - 1)
    slot_row = lax.broadcasted_iota(jnp.int32, (slots, cols), 0)
    slot_lane = lax.broadcasted_iota(jnp.int32, (slots, cols), 1)
    slot_level = jnp.where(slot_row < group, slot_row, slot_row - group) >> 1
    zero = jnp.zeros((rows, cols), jnp.float32)
    f32 = jnp.float32

    def slot_of(q, k):
        return group * (q % half) + 2 * k + q // half

    @pl.when(bottom)
    def _():
        row_in[:, SOUTH] = jnp.zeros_like(row_in[:, SOUTH])
        early_in[:, SOUTH] = jnp.zeros_like(early_in[:, SOUTH])
        row_side_in[:, :, SOUTH] = jnp.zeros_like(row_side_in[:, :, SOUTH])

    def remote(step, which, src, dst, peer):
        return pltpu.make_async_remote_copy(
            src_ref=src, dst_ref=dst, send_sem=send_sem.at[step, which],
            recv_sem=recv_sem.at[step, which], device_id=peer, device_id_type=MESH,
        )

    def col_copies(step):
        return [
            (remote(step, COL_E, col_out.at[step, EAST], col_in.at[step, WEST], east[0]), None),
            (remote(step, COL_W, col_out.at[step, WEST], col_in.at[step, EAST], west[0]), None),
        ]

    def row_pair(step, which_n, which_s, out, into, section):
        north_in, south_in = into(NORTH), into(SOUTH)
        peer_n, peer_s = north[section], south[section]
        return [
            (remote(step, which_n, out.at[step, NORTH], north_in, peer_n), top),
            (remote(step, which_s, out.at[step, NORTH], south_in, peer_n), jnp.logical_not(top)),
            (remote(step, which_n, out.at[step, SOUTH], north_in, peer_s), jnp.logical_not(bottom)),
        ]

    def row_copies():
        return row_pair(0, ROW_N, ROW_S, row_out, lambda side: row_in.at[0, side], 0)

    def early_copies():
        return row_pair(0, EARLY_N, EARLY_S, early_out, lambda side: early_in.at[0, side], 0)

    def side_copies(step):
        copies = []
        for section, names in enumerate(((SIDE_E, SIDE_W, SIDE_N, SIDE_S), (CROSS_E, CROSS_W, CROSS_N, CROSS_S))):
            for which, side, peer in ((names[0], EAST, east), (names[1], WEST, west)):
                copies.append((remote(
                    step, which, col_side_out.at[step, side], col_side_in.at[step, section, 1 - side], peer[section]
                ), None))
            copies += row_pair(
                step, names[2], names[3], row_side_out, lambda side: row_side_in.at[step, section, side], section
            )
        return copies

    def start(copies):
        for copy, go in copies:
            if go is None:
                copy.start()
            else:
                pl.when(go)(copy.start)

    def start_rows(copies):
        odd_lat = lax.rem(lat, 2) == 1
        even_lat = jnp.logical_not(odd_lat)
        start([(copy, jnp.logical_and(go, odd_lat)) for copy, go in copies[:2]])
        start(copies[2:])
        start([(copy, jnp.logical_and(go, even_lat)) for copy, go in copies[:2]])

    def wait_recv(copies):
        rest = []
        for copy, go in copies:
            if go is None:
                copy.wait_recv()
            else:
                rest.append(copy)
        for i in range(0, len(rest), 3):
            rest[i].wait_recv()
            pl.when(jnp.logical_not(bottom))(rest[i + 1].wait_recv)

    def pack(packed, q, k, value):
        slot, spot = q // half, (q % half) * levels + k
        turned = pltpu.roll(value, 2 * spot + 1, 1)
        packed = list(packed)
        packed[slot] = jnp.where((lane >> 1) == spot, turned, packed[slot])
        return tuple(packed)

    def gather(packed, src, lower, upper):
        for k in range(lower, upper):
            for q in range(fields):
                packed = pack(packed, q, k, src[q, k])
        return packed

    def split(packed):
        east_side = jnp.where(odd, pltpu.roll(packed[1], 1, 1), packed[0])
        west_side = jnp.where(odd, packed[1], pltpu.roll(packed[0], cols - 1, 1))
        return east_side, west_side

    def joined(from_west, from_east):
        first = jnp.where(odd, pltpu.roll(from_west, 1, 1), from_east)
        second = jnp.where(odd, from_west, pltpu.roll(from_east, cols - 1, 1))
        return first, second

    def take_row(src, side):
        flat = src.reshape(fields, levels * rows, cols)
        r = (rows - 1, 0)[side]
        for q in range(fields):
            row_own[side, pl.ds(slot_of(q, 0), levels, stride=2)] = flat[q, pl.ds(r, levels, stride=rows)]

    def row_coefs(moment, side):
        diff_rows, vel_rows = diff.reshape(steps, levels * rows, cols), vel.reshape(steps, 2, levels * rows, cols)
        r, sign = ((rows - 1, -1.0), (0, 1.0))[side]
        line = pl.ds(r, levels, stride=rows)
        value = (diff_rows[moment, line] + sign * vel_rows[moment, 1, line]) * mask_f[r:r + 1]
        for g in range(half):
            for p in range(2):
                row_coef[moment * 2 + side, pl.ds(g * group + p, levels, stride=2)] = value

    def col_coefs(moment):
        packed = zero
        for k in range(levels):
            d, z = diff[moment, k] * mask_f[...], vel[moment, 0, k] * mask_f[...]
            both = d + jnp.where(lane == cols - 1, -z, z)
            turned = pltpu.roll(both, 2 * k + 1, 1)
            packed = jnp.where((lane >> 1) == k, turned, packed)
        for side, value in (
            (EAST, jnp.where(odd, pltpu.roll(packed, 1, 1), packed)),
            (WEST, jnp.where(odd, packed, pltpu.roll(packed, cols - 1, 1))),
        ):
            col_coef[moment, side] = jnp.where(low, value, pltpu.roll(value, group, 1))

    def edge_rates():
        inverse = 1.0 / depth[...].astype(f32)
        for side, c in ((EAST, cols - 1), (WEST, 0)):
            rate = zero
            for q in range(fields):
                own = jnp.broadcast_to((weight[q] * inverse)[:, c:c + 1], (rows, cols))
                rate = jnp.where(lane == slot_of(q, 0), own, rate)
            col_rate[side] = rate
            col_depth[side] = jnp.broadcast_to(depth[:, c:c + 1], (rows, cols))
        for side, r in ((NORTH, rows - 1), (SOUTH, 0)):
            for g in range(half):
                rate = jnp.zeros((8, cols), f32)
                for p in range(2):
                    own = weight[g + p * half, r:r + 1] * inverse[r:r + 1]
                    rate = jnp.where(row8 == p, own, rate)
                row_rate[side, g] = rate

    def put_cols(step, moment, sides):
        for side, value in zip((EAST, WEST), sides):
            coef = col_coef[moment, side]
            col_out[step, side] = jnp.where(used, coef * value, pltpu.roll(coef, slots, 1))

    def put_row(moment, side, value):
        row_out[0, side, 0:slots] = row_coef[moment * 2 + side] * value
        row_out[0, side, slots:slots + 8] = row_coef[moment * 2 + side, 0:8]

    def put_early(moment, side, value):
        early_out[0, side, 0:slots] = row_coef[moment * 2 + side] * value
        early_out[0, side, slots:slots + group] = row_coef[moment * 2 + side, 0:group]

    def put_sides(step, col_sides, row_sides, ends=None):
        col_given = []
        for side, value in zip((EAST, WEST), col_sides):
            total = jnp.where(jnp.logical_and(used, lane_level < col_depth[side]), value, 0.0)
            turns = [pltpu.roll(total, cols - n, 1) for n in (2, 4, 6)]
            total = (total + turns[0]) + (turns[1] + turns[2])
            turns = [pltpu.roll(total, cols - n, 1) for n in (8, 16, 24, 32, 40)]
            total = ((total + turns[0]) + (turns[1] + turns[2])) + (turns[3] + turns[4])
            given = col_rate[side] * total
            col_given.append(given)
            out = given[0:8]
            for i in range(1, rows // 8):
                out = out + pltpu.roll(given[8 * i:8 * i + 8], 2 * i, 1)
            col_side_out[step, side] = out
        for side, value, r in zip((NORTH, SOUTH), row_sides, (rows - 1, 0)):
            live = jnp.where(slot_level < depth[r:r + 1], value, 0.0)
            out = jnp.zeros((8, cols), f32)
            for g in range(half):
                total = live[g * group:g * group + 8]
                for i in range(8, group, 8):
                    total = total + live[g * group + i:g * group + i + 8]
                total = (total + pltpu.roll(total, 2, 0)) + (pltpu.roll(total, 4, 0) + pltpu.roll(total, 6, 0))
                given = row_rate[side, g] * total
                out = out + (pltpu.roll(given, 2 * g, 0) if g else given)
            if ends is not None:
                for way, c in ((EAST, cols - 1), (WEST, 0)):
                    line = jnp.broadcast_to(col_given[way][r:r + 1], (8, cols))
                    for g in range(half):
                        for p in range(2):
                            shift = (c - group * g - p) % cols
                            turned = pltpu.roll(line, shift, 1) if shift else line
                            out = jnp.where(jnp.logical_and(row8 == 2 * g + p, lane8 == c), turned, out)
                    out = jnp.where(row8 == 4 + way, row_corner[side, way:way + 1] * ends[way][r:r + 1], out)
            row_side_out[step, side] = out

    def receive_cols(step):
        got = []
        for side in (EAST, WEST):
            value = col_in[step, side]
            coef = jnp.where(low, pltpu.roll(value, cols - slots, 1), pltpu.roll(value, cols - slots + group, 1))
            given = col_side_in[step, 1, side] - col_side_in[step, 0, side]
            given = jnp.concatenate(
                [given] + [pltpu.roll(given, cols - 2 * i, 1) for i in range(1, rows // 8)], axis=0
            )
            term = jnp.where(lane_level == 0, coef * given, 0.0)
            got.append(jnp.where(used, value + term, 0.0))
        return got

    def mirrored(value):
        at = lax.broadcasted_iota(jnp.int32, value.shape, 1)
        return jnp.take_along_axis(value, cols - 1 - at, axis=1)

    def receive_rows(step, main):
        for side in (NORTH, SOUTH):
            given = row_side_in[step, 1, side] - row_side_in[step, 0, side]
            coef = main[0, side, slots:slots + 1]
            for g in range(half):
                block = slice(g * group, g * group + 8)
                term = pltpu.roll(given, 8 - 2 * g, 0) if g else given
                term = jnp.where(row8 < 2, coef * term, 0.0)
                row_got[side, block] = main[0, side, block] + term
                block = slice(g * group + 8, (g + 1) * group)
                row_got[side, block] = main[0, side, block]

        @pl.when(top)
        def _():
            turned = mirrored(row_got[NORTH])
            row_got[NORTH] = jnp.where((slot_row & 1) == 1, -turned, turned)

    def receive_late(step, got):
        receive_rows(step, early_in)

        @pl.when(top)
        def _():
            early_in[0, NORTH, slots:slots + group] = mirrored(early_in[0, NORTH, slots:slots + group])

        for side in (NORTH, SOUTH):
            for g in range(half):
                block = slice(g * group, (g + 1) * group)
                more = early_in[0, side, slots:slots + group] * row_keep[side, block]
                row_got[side, block] = row_got[side, block] + more
        lines = [[row_side_in[step, 0, side, 4 + way:5 + way] for way in (EAST, WEST)] for side in (NORTH, SOUTH)]
        folded = [jnp.where(odd[0:1], -line, line) for line in lines[NORTH][::-1]]
        out = []
        for way, value in zip((EAST, WEST), got):
            line = jnp.where(top, folded[way], lines[NORTH][way])
            value = value + jnp.where(row == rows - 1, line, 0.0)
            out.append(value + jnp.where(row == 0, lines[SOUTH][way], 0.0))
        return out

    def col_corner(value):
        out = []
        for c in (cols - 1, 0):
            whole = jnp.broadcast_to(value[:, c:c + 1], (slots, cols))
            whole = jnp.where(slot_lane == slot_row, whole, 0.0)
            out.append(jnp.sum(whole, axis=0, keepdims=True))
        return out

    def interior(moment, k, src, dst, first=False, last=False):
        mask = mask_f[...]
        d, z, b = diff[moment, k] * mask, vel[moment, 0, k] * mask, vel[moment, 1, k] * mask
        own = mask - 4.0 * d - 2.0 * (mix[moment, k] * mask)
        above = None if first else mix[moment, k - 1] * mask
        below = None if last else mix[moment, k + 1] * mask
        eastward = jnp.where(lane == cols - 1, 0.0, d - z)
        westward = jnp.where(lane == 0, 0.0, d + z)
        northward = jnp.where(row == rows - 1, 0.0, d - b)
        southward = jnp.where(row == 0, 0.0, d + b)
        for q in range(fields):
            a = src[q, k]
            total = own * a
            if not first:
                total = total + above * src[q, k - 1]
            if not last:
                total = total + below * src[q, k + 1]
            total = total + pltpu.roll(eastward * a, 1, 1) + pltpu.roll(westward * a, cols - 1, 1)
            total = total + pltpu.roll(northward * a, 1, 0) + pltpu.roll(southward * a, rows - 1, 0)
            dst[q, k] = total

    for copy in first:
        copy.wait()
    mask_f[...] = mask_i[...].astype(f32)
    edge_rates()
    for side in (NORTH, SOUTH):
        for copy in parts[side]:
            copy.wait()
        take_row(field_a, side)
        row_coefs(steps - 1, side)
        put_row(steps - 1, side, row_own[side])

    @pl.when(bottom)
    def _():
        pl.semaphore_wait(barrier, 7)

    @pl.when(jnp.logical_not(bottom))
    def _():
        pl.semaphore_wait(barrier, 9)

    row_halo = row_copies()
    start_rows(row_halo)
    for copy in parts[2]:
        copy.wait()
    own_cols = split(gather((zero, zero), field_a, 0, levels))
    col_coefs(steps - 1)
    put_cols(0, steps - 1, own_cols)
    col_halo = col_copies(0)
    start(col_halo)
    put_sides(0, own_cols, (row_own[NORTH], row_own[SOUTH]))
    side_halo = side_copies(0)
    start(side_halo)
    halo = row_halo + col_halo + side_halo
    pending = halo

    def add(k, sums):
        live = k < depth[...]
        return tuple(s + jnp.where(live, field_a[q, k], 0.0) for q, s in enumerate(sums))

    sums = levels_loop(0, levels, add, (zero,) * fields, SUM)
    last_mix.wait()

    for step in range(steps):
        moment = steps - 1 - step
        src, dst = (field_a, field_b) if step % 2 == 0 else (field_b, field_a)
        final = step == steps - 1
        if final:
            dst = out_v.at[0]
        scale = 1.0 / depth[...].astype(f32)
        for q in range(fields):
            share[step, q] = weight[q] * (scale * sums[q])
        couple = remote(step, COUPLE, share.at[step], flux.at[step], partner)
        couple.start()
        pending = pending + [(couple, None)]

        def inner(k, carry, **ends):
            interior(moment, k, src, dst, **ends)
            return carry

        levels_loop(2, levels - 1, inner, 0, INNER)
        inner(levels - 1, 0, last=True)
        couple.wait_recv()
        for q in range(fields):
            src[q, 0] = src[q, 0] + (flux[step, q] - share[step, q])
        inner(0, 0, first=True)
        inner(1, 0)
        if not final:
            for copy in coeffs[moment - 1]:
                copy.wait()
            for side in (NORTH, SOUTH):
                take_row(dst, side)
                row_coefs(moment - 1, side)
                put_early(moment - 1, side, row_own[side])
            early = early_copies()
            start_rows(early)
            own_e, own_w = split(gather((zero, zero), dst, 0, levels))
            col_coefs(moment - 1)
            for side, r in ((NORTH, rows - 1), (SOUTH, 0)):
                for way, line in enumerate(col_corner(row_coef[2 * (moment - 1) + side])):
                    row_corner[side, way:way + 1] = line
                row_keep[side] = row_out[0, side, 0:slots]
                for q in range(fields):
                    at = slice(slot_of(q, 0), slot_of(q, 0) + 1)
                    row_keep[side, at] = row_coef[2 * moment + side, at] * src[q, 0, r:r + 1]

        wait_recv(halo)
        got_e, got_w = receive_cols(step)
        if final:
            got_e, got_w = receive_late(step, (got_e, got_w))
        else:
            receive_rows(step, row_in)
            col_more = [col_corner(row_got[side]) for side in (NORTH, SOUTH)]
            col_sides = []
            for side, value in ((EAST, own_e + got_e), (WEST, own_w + got_w)):
                value = value + jnp.where(row == rows - 1, col_more[NORTH][side], 0.0)
                col_sides.append(value + jnp.where(row == 0, col_more[SOUTH][side], 0.0))
            put_cols(step + 1, moment - 1, col_sides)
            col_halo = col_copies(step + 1)
            start(col_halo)
            row_sides = [row_own[side] + row_got[side] for side in (NORTH, SOUTH)]
            put_sides(step + 1, col_sides, row_sides, (got_e, got_w))
            side_halo = side_copies(step + 1)
            start(side_halo)
            halo = early + col_halo + side_halo
            pending = pending + halo

        pair = joined(got_w, got_e)
        if final:
            pair_v[0], pair_v[1] = pair
            break

        sums = [zero] * fields
        for k in range(levels):
            for q in range(fields):
                total = finished(dst[q, k], pair[q // half], row_got, (q % half) * levels + k, slot_of(q, k))
                dst[q, k] = total
                sums[q] = sums[q] + jnp.where(k < depth[...], total, 0.0)

    for copy, go in pending:
        if go is None:
            copy.wait_send()
        else:
            pl.when(go)(copy.wait_send)


def solution(mesh):
    lats, lons = mesh.shape["lat"], mesh.shape["lon"]

    def shards(adjoint, land_mask, coupling_depth, coupling_weight, diffusion, velocity, mixing):
        _, fields, levels, rows, cols = adjoint.shape
        steps = diffusion.shape[0]
        f32 = jnp.float32
        block = (rows, cols)
        slots = fields * levels
        column = pltpu.VMEM((steps, 2, rows, cols), f32)
        edge = pltpu.VMEM((1, 2, slots + 8, cols), f32)
        early = pltpu.VMEM((1, 2, slots + 2 * levels, cols), f32)
        side_out, side_in = pltpu.VMEM((steps, 2, 8, cols), f32), pltpu.VMEM((steps, 2, 2, 8, cols), f32)
        parts = pl.pallas_call(
            functools.partial(kernel, lats, lons),
            out_shape=(
                jax.ShapeDtypeStruct(adjoint.shape, f32),
                jax.ShapeDtypeStruct((2, rows, cols), f32),
                jax.ShapeDtypeStruct((2, slots, cols), f32),
            ),
            in_specs=[pl.BlockSpec(memory_space=pltpu.HBM)] * 7,
            out_specs=(pl.BlockSpec(memory_space=pltpu.VMEM),) * 3,
            scratch_shapes=[
                pltpu.VMEM((fields, levels, rows, cols), f32),
                pltpu.VMEM((fields, levels, rows, cols), f32),
                pltpu.VMEM((steps, levels, rows, cols), f32),
                pltpu.VMEM((steps, 2, levels, rows, cols), f32),
                pltpu.VMEM((steps, levels, rows, cols), f32),
                pltpu.VMEM(block, jnp.int32),
                pltpu.VMEM(block, jnp.int32),
                pltpu.VMEM((fields, rows, cols), f32),
                pltpu.VMEM(block, f32),
                pltpu.VMEM((steps, fields, rows, cols), f32),
                pltpu.VMEM((steps, fields, rows, cols), f32),
                pltpu.VMEM((2, rows, cols), jnp.int32),
                pltpu.VMEM((2, rows, cols), f32),
                column,
                pltpu.VMEM((2, fields // 2, 8, cols), f32),
                pltpu.VMEM((steps * 2, slots, cols), f32),
                pltpu.VMEM((2, slots, cols), f32),
                pltpu.VMEM((2, slots, cols), f32),
                pltpu.VMEM((2, 8, cols), f32),
                early, early,
                column, column, side_out, side_in,
                edge, edge, side_out, side_in,
                pltpu.SemaphoreType.DMA((10 + 3 * steps,)),
                pltpu.SemaphoreType.DMA((steps, COPIES)),
                pltpu.SemaphoreType.DMA((steps, COPIES)),
            ],
            compiler_params=pltpu.CompilerParams(
                collective_id=0, has_side_effects=True, vmem_limit_bytes=40 * 1024 * 1024
            ),
            name="adjoint",
        )(*(pltpu.with_memory_space_constraint(x, pltpu.HBM) for x in (adjoint, land_mask, coupling_depth, coupling_weight, diffusion, velocity, mixing)))
        return pl.pallas_call(
            finish_kernel,
            out_shape=jax.ShapeDtypeStruct(adjoint.shape, f32),
            in_specs=[pl.BlockSpec(memory_space=pltpu.VMEM)] * 3,
            out_specs=pl.BlockSpec(memory_space=pltpu.HBM),
            scratch_shapes=[
                pltpu.VMEM((fields, levels, rows, cols), f32), pltpu.SemaphoreType.DMA((PIECES * fields,)),
            ],
            compiler_params=pltpu.CompilerParams(vmem_limit_bytes=16 * 1024 * 1024),
            name="adjoint_finish",
        )(*parts)

    in_specs = (
        P("ice", None, None, "lat", "lon"),
        P("lat", "lon"),
        P("ice", "lat", "lon"),
        P("ice", None, "lat", "lon"),
        P(None, "ice", None, "lat", "lon"),
        P(None, "ice", None, None, "lat", "lon"),
        P(None, "ice", None, "lat", "lon"),
    )
    out_specs = P("ice", None, None, "lat", "lon")
    return jax.shard_map(shards, mesh=mesh, in_specs=in_specs, out_specs=out_specs, check_vma=False)
```

```python
import functools

import jax
import jax.numpy as jnp
from jax import lax
from jax.experimental import pallas as pl
from jax.experimental.pallas import tpu as pltpu
from jax.sharding import PartitionSpec as P

MESH = pl.DeviceIdType.MESH
INNER, SUM, PIECES = 7, 4, 2
COUPLE, COL_E, COL_W, ROW_N, ROW_S, SIDE_E, SIDE_W, SIDE_N, SIDE_S, CROSS_E, CROSS_W, CROSS_N, CROSS_S, EARLY_N, EARLY_S = range(15)
COPIES = 15
EAST, WEST, NORTH, SOUTH = 0, 1, 0, 1


def levels_loop(lower, upper, body, carry, times):
    whole = (upper - lower) // times

    def some(i, carry):
        for j in range(times):
            carry = body(lower + i * times + j, carry)
        return carry

    if whole > 0:
        carry = lax.fori_loop(0, whole, some, carry)
    for k in range(lower + whole * times, upper):
        carry = body(k, carry)
    return carry


def finished(value, pair, row_got, spot, slot):
    rows, cols = value.shape
    lane8 = lax.broadcasted_iota(jnp.int32, (8, cols), 1)
    row8 = lax.broadcasted_iota(jnp.int32, (8, cols), 0)
    ends8 = jnp.logical_or(lane8 == 0, lane8 == cols - 1)
    parts = []
    for r in range(0, rows, 8):
        turned = pltpu.roll(pair[r:r + 8], cols - 1 - 2 * spot, 1)
        total = value[r:r + 8] + jnp.where(ends8, turned, 0.0)
        if r == 0:
            total = total + jnp.where(row8 == 0, row_got[SOUTH, slot:slot + 1], 0.0)
        if r == rows - 8:
            total = total + jnp.where(row8 == 7, row_got[NORTH, slot:slot + 1], 0.0)
        parts.append(total)
    return jnp.concatenate(parts, axis=0)


def finish_kernel(value, pair, row_got, out_h, done, sems):
    _, fields, levels, rows, cols = value.shape
    half = fields // 2
    pairs = [pair[i] for i in range(half)]
    pieces = sems.shape[0] // fields
    span = levels // pieces
    copies = []
    for q in range(fields):
        for k in range(levels):
            slot = 2 * levels * (q % half) + 2 * k + q // half
            done[q, k] = finished(value[0, q, k], pairs[q // half], row_got, (q % half) * levels + k, slot)
            if (k + 1) % span == 0:
                part = pl.ds(k + 1 - span, span)
                copies.append(pltpu.make_async_copy(done.at[q, part], out_h.at[0, q, part], sems.at[len(copies)]))
                copies[-1].start()
    for copy in copies:
        copy.wait()


def kernel(
    lats, lons, adj_h, mask_h, depth_h, weight_h, diff_h, vel_h, mix_h,
    out_v, pair_v, row_got,
    field_a, field_b, diff, vel, mix, mask_i, depth, weight, mask_f,
    share, flux, col_depth, col_rate, col_coef, row_rate, row_coef, row_own, row_keep, row_corner, early_out, early_in,
    col_out, col_in, col_side_out, col_side_in, row_out, row_in, row_side_out, row_side_in,
    load_sem, send_sem, recv_sem,
):
    fields, levels, rows, cols = field_a.shape
    steps = diff.shape[0]
    half = fields // 2
    group = 2 * levels
    slots = fields * levels
    ice, lat, lon = lax.axis_index("ice"), lax.axis_index("lat"), lax.axis_index("lon")
    top, bottom = lat == lats - 1, lat == 0
    lon_e, lon_w = lax.rem(lon + 1, lons), lax.rem(lon + lons - 1, lons)
    lat_n = jnp.where(top, lat, lat + 1)
    lon_n = jnp.where(top, lons - 1 - lon, lon)
    lat_s = jnp.where(bottom, 0, lat - 1)
    partner = (1 - ice, lat, lon)
    east, west, north, south = [
        [(section, y, x) for section in (ice, 1 - ice)]
        for y, x in ((lat, lon_e), (lat, lon_w), (lat_n, lon_n), (lat_s, lon))
    ]

    barrier = pltpu.get_barrier_semaphore()
    for peer in [partner] + east + west + north:
        pl.semaphore_signal(barrier, inc=1, device_id=peer, device_id_type=MESH)

    @pl.when(jnp.logical_not(bottom))
    def _():
        for peer in south:
            pl.semaphore_signal(barrier, inc=1, device_id=peer, device_id_type=MESH)

    first = [
        pltpu.make_async_copy(depth_h.at[0], depth, load_sem.at[0]),
        pltpu.make_async_copy(weight_h.at[0], weight, load_sem.at[1]),
        pltpu.make_async_copy(mask_h, mask_i, load_sem.at[2]),
    ]
    coeffs = []
    for moment in range(steps - 1):
        base = 12 + 3 * moment
        coeffs.append([
            pltpu.make_async_copy(diff_h.at[moment, 0], diff.at[moment], load_sem.at[base]),
            pltpu.make_async_copy(vel_h.at[moment, 0], vel.at[moment], load_sem.at[base + 1]),
            pltpu.make_async_copy(mix_h.at[moment, 0], mix.at[moment], load_sem.at[base + 2]),
        ])
    moment = steps - 1
    last_mix = pltpu.make_async_copy(mix_h.at[moment, 0], mix.at[moment], load_sem.at[12 + 3 * moment])
    parts = []
    for i, (r, n) in enumerate(((rows - 8, 8), (0, 8), (8, rows - 16))):
        part = pl.ds(r, n)
        parts.append([
            pltpu.make_async_copy(adj_h.at[0, :, :, part], field_a.at[:, :, part], load_sem.at[3 + i]),
            pltpu.make_async_copy(diff_h.at[moment, 0, :, part], diff.at[moment, :, part], load_sem.at[6 + i]),
            pltpu.make_async_copy(vel_h.at[moment, 0, :, :, part], vel.at[moment, :, :, part], load_sem.at[9 + i]),
        ])
    for copies in [first] + parts + [[last_mix]] + coeffs[::-1]:
        for copy in copies:
            copy.start()

    lane = lax.broadcasted_iota(jnp.int32, (rows, cols), 1)
    row = lax.broadcasted_iota(jnp.int32, (rows, cols), 0)
    odd = (lane & 1) == 1
    low = lane < group
    used = lane < slots
    lane_level = jnp.where(low, lane, lane - group) >> 1
    lane8 = lax.broadcasted_iota(jnp.int32, (8, cols), 1)
    row8 = lax.broadcasted_iota(jnp.int32, (8, cols), 0)
    ends8 = jnp.logical_or(lane8 == 0, lane8 == cols - 1)
    slot_row = lax.broadcasted_iota(jnp.int32, (slots, cols), 0)
    slot_lane = lax.broadcasted_iota(jnp.int32, (slots, cols), 1)
    slot_level = jnp.where(slot_row < group, slot_row, slot_row - group) >> 1
    zero = jnp.zeros((rows, cols), jnp.float32)
    f32 = jnp.float32

    def slot_of(q, k):
        return group * (q % half) + 2 * k + q // half

    @pl.when(bottom)
    def _():
        row_in[:, SOUTH] = jnp.zeros_like(row_in[:, SOUTH])
        early_in[:, SOUTH] = jnp.zeros_like(early_in[:, SOUTH])
        row_side_in[:, :, SOUTH] = jnp.zeros_like(row_side_in[:, :, SOUTH])

    def remote(step, which, src, dst, peer):
        return pltpu.make_async_remote_copy(
            src_ref=src, dst_ref=dst, send_sem=send_sem.at[step, which],
            recv_sem=recv_sem.at[step, which], device_id=peer, device_id_type=MESH,
        )

    def col_copies(step):
        return [
            (remote(step, COL_E, col_out.at[step, EAST], col_in.at[step, WEST], east[0]), None),
            (remote(step, COL_W, col_out.at[step, WEST], col_in.at[step, EAST], west[0]), None),
        ]

    def row_pair(step, which_n, which_s, out, into, section):
        north_in, south_in = into(NORTH), into(SOUTH)
        peer_n, peer_s = north[section], south[section]
        return [
            (remote(step, which_n, out.at[step, NORTH], north_in, peer_n), top),
            (remote(step, which_s, out.at[step, NORTH], south_in, peer_n), jnp.logical_not(top)),
            (remote(step, which_n, out.at[step, SOUTH], north_in, peer_s), jnp.logical_not(bottom)),
        ]

    def row_copies():
        return row_pair(0, ROW_N, ROW_S, row_out, lambda side: row_in.at[0, side], 0)

    def early_copies():
        return row_pair(0, EARLY_N, EARLY_S, early_out, lambda side: early_in.at[0, side], 0)

    def side_copies(step):
        copies = []
        for section, names in enumerate(((SIDE_E, SIDE_W, SIDE_N, SIDE_S), (CROSS_E, CROSS_W, CROSS_N, CROSS_S))):
            for which, side, peer in ((names[0], EAST, east), (names[1], WEST, west)):
                copies.append((remote(
                    step, which, col_side_out.at[step, side], col_side_in.at[step, section, 1 - side], peer[section]
                ), None))
            copies += row_pair(
                step, names[2], names[3], row_side_out, lambda side: row_side_in.at[step, section, side], section
            )
        return copies

    def start(copies):
        for copy, go in copies:
            if go is None:
                copy.start()
            else:
                pl.when(go)(copy.start)

    def start_rows(copies):
        odd_lat = lax.rem(lat, 2) == 1
        even_lat = jnp.logical_not(odd_lat)
        start([(copy, jnp.logical_and(go, odd_lat)) for copy, go in copies[:2]])
        start(copies[2:])
        start([(copy, jnp.logical_and(go, even_lat)) for copy, go in copies[:2]])

    def wait_recv(copies):
        rest = []
        for copy, go in copies:
            if go is None:
                copy.wait_recv()
            else:
                rest.append(copy)
        for i in range(0, len(rest), 3):
            rest[i].wait_recv()
            pl.when(jnp.logical_not(bottom))(rest[i + 1].wait_recv)

    def pack(packed, q, k, value):
        slot, spot = q // half, (q % half) * levels + k
        turned = pltpu.roll(value, 2 * spot + 1, 1)
        packed = list(packed)
        packed[slot] = jnp.where((lane >> 1) == spot, turned, packed[slot])
        return tuple(packed)

    def gather(packed, src, lower, upper):
        for k in range(lower, upper):
            for q in range(fields):
                packed = pack(packed, q, k, src[q, k])
        return packed

    def split(packed):
        east_side = jnp.where(odd, pltpu.roll(packed[1], 1, 1), packed[0])
        west_side = jnp.where(odd, packed[1], pltpu.roll(packed[0], cols - 1, 1))
        return east_side, west_side

    def joined(from_west, from_east):
        first = jnp.where(odd, pltpu.roll(from_west, 1, 1), from_east)
        second = jnp.where(odd, from_west, pltpu.roll(from_east, cols - 1, 1))
        return first, second

    def take_row(src, side):
        flat = src.reshape(fields, levels * rows, cols)
        r = (rows - 1, 0)[side]
        for q in range(fields):
            row_own[side, pl.ds(slot_of(q, 0), levels, stride=2)] = flat[q, pl.ds(r, levels, stride=rows)]

    def row_local(moment, side, src):
        flat = src.reshape(fields, levels * rows, cols)
        diff_rows, mix_rows = diff.reshape(steps, levels * rows, cols), mix.reshape(steps, levels * rows, cols)
        vel_rows = vel.reshape(steps, 2, levels * rows, cols)
        r, inner, sign = ((rows - 1, rows - 2, -1.0), (0, 1, 1.0))[side]
        line, near = pl.ds(r, levels, stride=rows), pl.ds(inner, levels, stride=rows)
        level = lax.broadcasted_iota(jnp.int32, (levels, cols), 0)
        at = lax.broadcasted_iota(jnp.int32, (levels, cols), 1)
        m = mask_f[r:r + 1]
        d, z, v = diff_rows[moment, line] * m, vel_rows[moment, 0, line] * m, mix_rows[moment, line] * m
        own = m - 4.0 * d - 2.0 * v
        eastward = jnp.where(at == cols - 1, 0.0, d - z)
        westward = jnp.where(at == 0, 0.0, d + z)
        inward = (diff_rows[moment, near] + sign * vel_rows[moment, 1, near]) * mask_f[inner:inner + 1]
        for q in range(fields):
            a = flat[q, line]
            total = own * a + inward * flat[q, near]
            total = total + jnp.where(level == 0, 0.0, pltpu.roll(v * a, 1, 0))
            total = total + jnp.where(level == levels - 1, 0.0, pltpu.roll(v * a, levels - 1, 0))
            total = total + pltpu.roll(eastward * a, 1, 1) + pltpu.roll(westward * a, cols - 1, 1)
            row_own[side, pl.ds(slot_of(q, 0), levels, stride=2)] = total

    def row_coefs(moment, side):
        diff_rows, vel_rows = diff.reshape(steps, levels * rows, cols), vel.reshape(steps, 2, levels * rows, cols)
        r, sign = ((rows - 1, -1.0), (0, 1.0))[side]
        line = pl.ds(r, levels, stride=rows)
        value = (diff_rows[moment, line] + sign * vel_rows[moment, 1, line]) * mask_f[r:r + 1]
        for g in range(half):
            for p in range(2):
                row_coef[moment * 2 + side, pl.ds(g * group + p, levels, stride=2)] = value

    def col_coefs(moment):
        packed = zero
        for k in range(levels):
            d, z = diff[moment, k] * mask_f[...], vel[moment, 0, k] * mask_f[...]
            both = d + jnp.where(lane == cols - 1, -z, z)
            turned = pltpu.roll(both, 2 * k + 1, 1)
            packed = jnp.where((lane >> 1) == k, turned, packed)
        for side, value in (
            (EAST, jnp.where(odd, pltpu.roll(packed, 1, 1), packed)),
            (WEST, jnp.where(odd, packed, pltpu.roll(packed, cols - 1, 1))),
        ):
            col_coef[moment, side] = jnp.where(low, value, pltpu.roll(value, group, 1))

    def edge_rates():
        inverse = 1.0 / depth[...].astype(f32)
        for side, c in ((EAST, cols - 1), (WEST, 0)):
            rate = zero
            for q in range(fields):
                own = jnp.broadcast_to((weight[q] * inverse)[:, c:c + 1], (rows, cols))
                rate = jnp.where(lane == slot_of(q, 0), own, rate)
            col_rate[side] = rate
            col_depth[side] = jnp.broadcast_to(depth[:, c:c + 1], (rows, cols))
        for side, r in ((NORTH, rows - 1), (SOUTH, 0)):
            for g in range(half):
                rate = jnp.zeros((8, cols), f32)
                for p in range(2):
                    own = weight[g + p * half, r:r + 1] * inverse[r:r + 1]
                    rate = jnp.where(row8 == p, own, rate)
                row_rate[side, g] = rate

    def put_cols(step, moment, sides):
        for side, value in zip((EAST, WEST), sides):
            coef = col_coef[moment, side]
            col_out[step, side] = jnp.where(used, coef * value, pltpu.roll(coef, slots, 1))

    def put_row(moment, side, value):
        row_out[0, side, 0:slots] = row_coef[moment * 2 + side] * value
        row_out[0, side, slots:slots + 8] = row_coef[moment * 2 + side, 0:8]

    def put_early(moment, side, value):
        early_out[0, side, 0:slots] = row_coef[moment * 2 + side] * value
        early_out[0, side, slots:slots + group] = row_coef[moment * 2 + side, 0:group]

    def put_sides(step, col_sides, row_sides, ends=None):
        col_given = []
        for side, value in zip((EAST, WEST), col_sides):
            total = jnp.where(jnp.logical_and(used, lane_level < col_depth[side]), value, 0.0)
            turns = [pltpu.roll(total, cols - n, 1) for n in (2, 4, 6)]
            total = (total + turns[0]) + (turns[1] + turns[2])
            turns = [pltpu.roll(total, cols - n, 1) for n in (8, 16, 24, 32, 40)]
            total = ((total + turns[0]) + (turns[1] + turns[2])) + (turns[3] + turns[4])
            given = col_rate[side] * total
            col_given.append(given)
            out = given[0:8]
            for i in range(1, rows // 8):
                out = out + pltpu.roll(given[8 * i:8 * i + 8], 2 * i, 1)
            col_side_out[step, side] = out
        for side, value, r in zip((NORTH, SOUTH), row_sides, (rows - 1, 0)):
            live = jnp.where(slot_level < depth[r:r + 1], value, 0.0)
            out = jnp.zeros((8, cols), f32)
            for g in range(half):
                total = live[g * group:g * group + 8]
                for i in range(8, group, 8):
                    total = total + live[g * group + i:g * group + i + 8]
                total = (total + pltpu.roll(total, 2, 0)) + (pltpu.roll(total, 4, 0) + pltpu.roll(total, 6, 0))
                given = row_rate[side, g] * total
                out = out + (pltpu.roll(given, 2 * g, 0) if g else given)
            if ends is not None:
                for way, c in ((EAST, cols - 1), (WEST, 0)):
                    line = jnp.broadcast_to(col_given[way][r:r + 1], (8, cols))
                    for g in range(half):
                        for p in range(2):
                            shift = (c - group * g - p) % cols
                            turned = pltpu.roll(line, shift, 1) if shift else line
                            out = jnp.where(jnp.logical_and(row8 == 2 * g + p, lane8 == c), turned, out)
                    out = jnp.where(row8 == 4 + way, row_corner[side, way:way + 1] * ends[way][r:r + 1], out)
            row_side_out[step, side] = out

    def receive_cols(step):
        got = []
        for side in (EAST, WEST):
            value = col_in[step, side]
            coef = jnp.where(low, pltpu.roll(value, cols - slots, 1), pltpu.roll(value, cols - slots + group, 1))
            given = col_side_in[step, 1, side] - col_side_in[step, 0, side]
            given = jnp.concatenate(
                [given] + [pltpu.roll(given, cols - 2 * i, 1) for i in range(1, rows // 8)], axis=0
            )
            term = jnp.where(lane_level == 0, coef * given, 0.0)
            got.append(jnp.where(used, value + term, 0.0))
        return got

    def mirrored(value):
        at = lax.broadcasted_iota(jnp.int32, value.shape, 1)
        return jnp.take_along_axis(value, cols - 1 - at, axis=1)

    def receive_rows(step, main):
        for side in (NORTH, SOUTH):
            given = row_side_in[step, 1, side] - row_side_in[step, 0, side]
            coef = main[0, side, slots:slots + 1]
            for g in range(half):
                block = slice(g * group, g * group + 8)
                term = pltpu.roll(given, 8 - 2 * g, 0) if g else given
                term = jnp.where(row8 < 2, coef * term, 0.0)
                row_got[side, block] = main[0, side, block] + term
                block = slice(g * group + 8, (g + 1) * group)
                row_got[side, block] = main[0, side, block]

        @pl.when(top)
        def _():
            turned = mirrored(row_got[NORTH])
            row_got[NORTH] = jnp.where((slot_row & 1) == 1, -turned, turned)

    def receive_late(step, got):
        receive_rows(step, early_in)

        @pl.when(top)
        def _():
            early_in[0, NORTH, slots:slots + group] = mirrored(early_in[0, NORTH, slots:slots + group])

        for side in (NORTH, SOUTH):
            for g in range(half):
                block = slice(g * group, (g + 1) * group)
                more = early_in[0, side, slots:slots + group] * row_keep[side, block]
                row_got[side, block] = row_got[side, block] + more
        lines = [[row_side_in[step, 0, side, 4 + way:5 + way] for way in (EAST, WEST)] for side in (NORTH, SOUTH)]
        folded = [jnp.where(odd[0:1], -line, line) for line in lines[NORTH][::-1]]
        out = []
        for way, value in zip((EAST, WEST), got):
            line = jnp.where(top, folded[way], lines[NORTH][way])
            value = value + jnp.where(row == rows - 1, line, 0.0)
            out.append(value + jnp.where(row == 0, lines[SOUTH][way], 0.0))
        return out

    def col_corner(value):
        out = []
        for c in (cols - 1, 0):
            whole = jnp.broadcast_to(value[:, c:c + 1], (slots, cols))
            whole = jnp.where(slot_lane == slot_row, whole, 0.0)
            out.append(jnp.sum(whole, axis=0, keepdims=True))
        return out

    def interior(moment, k, src, dst, first=False, last=False):
        mask = mask_f[...]
        d, z, b = diff[moment, k] * mask, vel[moment, 0, k] * mask, vel[moment, 1, k] * mask
        own = mask - 4.0 * d - 2.0 * (mix[moment, k] * mask)
        above = None if first else mix[moment, k - 1] * mask
        below = None if last else mix[moment, k + 1] * mask
        eastward = jnp.where(lane == cols - 1, 0.0, d - z)
        westward = jnp.where(lane == 0, 0.0, d + z)
        northward = jnp.where(row == rows - 1, 0.0, d - b)
        southward = jnp.where(row == 0, 0.0, d + b)
        for q in range(fields):
            a = src[q, k]
            total = own * a
            if not first:
                total = total + above * src[q, k - 1]
            if not last:
                total = total + below * src[q, k + 1]
            total = total + pltpu.roll(eastward * a, 1, 1) + pltpu.roll(westward * a, cols - 1, 1)
            total = total + pltpu.roll(northward * a, 1, 0) + pltpu.roll(southward * a, rows - 1, 0)
            dst[q, k] = total

    for copy in first:
        copy.wait()
    mask_f[...] = mask_i[...].astype(f32)
    edge_rates()
    for side in (NORTH, SOUTH):
        for copy in parts[side]:
            copy.wait()
        take_row(field_a, side)
        row_coefs(steps - 1, side)
        put_row(steps - 1, side, row_own[side])

    @pl.when(bottom)
    def _():
        pl.semaphore_wait(barrier, 7)

    @pl.when(jnp.logical_not(bottom))
    def _():
        pl.semaphore_wait(barrier, 9)

    row_halo = row_copies()
    start_rows(row_halo)
    for copy in parts[2]:
        copy.wait()
    own_cols = split(gather((zero, zero), field_a, 0, levels))
    col_coefs(steps - 1)
    put_cols(0, steps - 1, own_cols)
    col_halo = col_copies(0)
    start(col_halo)
    put_sides(0, own_cols, (row_own[NORTH], row_own[SOUTH]))
    side_halo = side_copies(0)
    start(side_halo)
    halo = row_halo + col_halo + side_halo
    pending = halo

    def add(k, sums):
        live = k < depth[...]
        return tuple(s + jnp.where(live, field_a[q, k], 0.0) for q, s in enumerate(sums))

    sums = levels_loop(0, levels, add, (zero,) * fields, SUM)
    last_mix.wait()

    for step in range(steps):
        moment = steps - 1 - step
        src, dst = (field_a, field_b) if step % 2 == 0 else (field_b, field_a)
        final = step == steps - 1
        if final:
            dst = out_v.at[0]
        scale = 1.0 / depth[...].astype(f32)
        for q in range(fields):
            share[step, q] = weight[q] * (scale * sums[q])
        couple = remote(step, COUPLE, share.at[step], flux.at[step], partner)
        couple.start()
        pending = pending + [(couple, None)]

        def inner(k, carry, **ends):
            interior(moment, k, src, dst, **ends)
            return carry

        split_at = levels - 1 if final else 2 + 2 * INNER
        levels_loop(2, split_at, inner, 0, INNER)
        if final:
            inner(levels - 1, 0, last=True)
        couple.wait_recv()
        for q in range(fields):
            src[q, 0] = src[q, 0] + (flux[step, q] - share[step, q])
        if not final:
            for copy in coeffs[moment - 1]:
                copy.wait()
            for side in (NORTH, SOUTH):
                row_local(moment, side, src)
                row_coefs(moment - 1, side)
                put_early(moment - 1, side, row_own[side])
            early = early_copies()
            start_rows(early)
            levels_loop(split_at, levels - 1, inner, 0, INNER)
            inner(levels - 1, 0, last=True)
        inner(0, 0, first=True)
        inner(1, 0)
        if not final:
            own_e, own_w = split(gather((zero, zero), dst, 0, levels))
            col_coefs(moment - 1)
            for side, r in ((NORTH, rows - 1), (SOUTH, 0)):
                for way, line in enumerate(col_corner(row_coef[2 * (moment - 1) + side])):
                    row_corner[side, way:way + 1] = line
                row_keep[side] = row_out[0, side, 0:slots]
                for q in range(fields):
                    at = slice(slot_of(q, 0), slot_of(q, 0) + 1)
                    row_keep[side, at] = row_coef[2 * moment + side, at] * src[q, 0, r:r + 1]

        wait_recv(halo)
        got_e, got_w = receive_cols(step)
        if final:
            got_e, got_w = receive_late(step, (got_e, got_w))
        else:
            receive_rows(step, row_in)
            col_more = [col_corner(row_got[side]) for side in (NORTH, SOUTH)]
            col_sides = []
            for side, value in ((EAST, own_e + got_e), (WEST, own_w + got_w)):
                value = value + jnp.where(row == rows - 1, col_more[NORTH][side], 0.0)
                col_sides.append(value + jnp.where(row == 0, col_more[SOUTH][side], 0.0))
            put_cols(step + 1, moment - 1, col_sides)
            col_halo = col_copies(step + 1)
            start(col_halo)
            row_sides = [row_own[side] + row_got[side] for side in (NORTH, SOUTH)]
            put_sides(step + 1, col_sides, row_sides, (got_e, got_w))
            side_halo = side_copies(step + 1)
            start(side_halo)
            halo = early + col_halo + side_halo
            pending = pending + halo

        pair = joined(got_w, got_e)
        if final:
            pair_v[0], pair_v[1] = pair
            break

        sums = [zero] * fields
        for k in range(levels):
            for q in range(fields):
                total = finished(dst[q, k], pair[q // half], row_got, (q % half) * levels + k, slot_of(q, k))
                dst[q, k] = total
                sums[q] = sums[q] + jnp.where(k < depth[...], total, 0.0)

    for copy, go in pending:
        if go is None:
            copy.wait_send()
        else:
            pl.when(go)(copy.wait_send)


def solution(mesh):
    lats, lons = mesh.shape["lat"], mesh.shape["lon"]

    def shards(adjoint, land_mask, coupling_depth, coupling_weight, diffusion, velocity, mixing):
        _, fields, levels, rows, cols = adjoint.shape
        steps = diffusion.shape[0]
        f32 = jnp.float32
        block = (rows, cols)
        slots = fields * levels
        column = pltpu.VMEM((steps, 2, rows, cols), f32)
        edge = pltpu.VMEM((1, 2, slots + 8, cols), f32)
        early = pltpu.VMEM((1, 2, slots + 2 * levels, cols), f32)
        side_out, side_in = pltpu.VMEM((steps, 2, 8, cols), f32), pltpu.VMEM((steps, 2, 2, 8, cols), f32)
        parts = pl.pallas_call(
            functools.partial(kernel, lats, lons),
            out_shape=(
                jax.ShapeDtypeStruct(adjoint.shape, f32),
                jax.ShapeDtypeStruct((2, rows, cols), f32),
                jax.ShapeDtypeStruct((2, slots, cols), f32),
            ),
            in_specs=[pl.BlockSpec(memory_space=pltpu.HBM)] * 7,
            out_specs=(pl.BlockSpec(memory_space=pltpu.VMEM),) * 3,
            scratch_shapes=[
                pltpu.VMEM((fields, levels, rows, cols), f32),
                pltpu.VMEM((fields, levels, rows, cols), f32),
                pltpu.VMEM((steps, levels, rows, cols), f32),
                pltpu.VMEM((steps, 2, levels, rows, cols), f32),
                pltpu.VMEM((steps, levels, rows, cols), f32),
                pltpu.VMEM(block, jnp.int32),
                pltpu.VMEM(block, jnp.int32),
                pltpu.VMEM((fields, rows, cols), f32),
                pltpu.VMEM(block, f32),
                pltpu.VMEM((steps, fields, rows, cols), f32),
                pltpu.VMEM((steps, fields, rows, cols), f32),
                pltpu.VMEM((2, rows, cols), jnp.int32),
                pltpu.VMEM((2, rows, cols), f32),
                column,
                pltpu.VMEM((2, fields // 2, 8, cols), f32),
                pltpu.VMEM((steps * 2, slots, cols), f32),
                pltpu.VMEM((2, slots, cols), f32),
                pltpu.VMEM((2, slots, cols), f32),
                pltpu.VMEM((2, 8, cols), f32),
                early, early,
                column, column, side_out, side_in,
                edge, edge, side_out, side_in,
                pltpu.SemaphoreType.DMA((10 + 3 * steps,)),
                pltpu.SemaphoreType.DMA((steps, COPIES)),
                pltpu.SemaphoreType.DMA((steps, COPIES)),
            ],
            compiler_params=pltpu.CompilerParams(
                collective_id=0, has_side_effects=True, vmem_limit_bytes=40 * 1024 * 1024
            ),
            name="adjoint",
        )(*(pltpu.with_memory_space_constraint(x, pltpu.HBM) for x in (adjoint, land_mask, coupling_depth, coupling_weight, diffusion, velocity, mixing)))
        return pl.pallas_call(
            finish_kernel,
            out_shape=jax.ShapeDtypeStruct(adjoint.shape, f32),
            in_specs=[pl.BlockSpec(memory_space=pltpu.VMEM)] * 3,
            out_specs=pl.BlockSpec(memory_space=pltpu.HBM),
            scratch_shapes=[
                pltpu.VMEM((fields, levels, rows, cols), f32), pltpu.SemaphoreType.DMA((PIECES * fields,)),
            ],
            compiler_params=pltpu.CompilerParams(vmem_limit_bytes=16 * 1024 * 1024),
            name="adjoint_finish",
        )(*parts)

    in_specs = (
        P("ice", None, None, "lat", "lon"),
        P("lat", "lon"),
        P("ice", "lat", "lon"),
        P("ice", None, "lat", "lon"),
        P(None, "ice", None, "lat", "lon"),
        P(None, "ice", None, None, "lat", "lon"),
        P(None, "ice", None, "lat", "lon"),
    )
    out_specs = P("ice", None, None, "lat", "lon")
    return jax.shard_map(shards, mesh=mesh, in_specs=in_specs, out_specs=out_specs, check_vma=False)
```

```python
import functools

import jax
import jax.numpy as jnp
from jax import lax
from jax.experimental import pallas as pl
from jax.experimental.pallas import tpu as pltpu
from jax.sharding import PartitionSpec as P

MESH = pl.DeviceIdType.MESH
INNER, SUM, PIECES = 7, 4, 2
COUPLE, COL_E, COL_W, ROW_N, ROW_S, SIDE_E, SIDE_W, SIDE_N, SIDE_S, CROSS_E, CROSS_W, CROSS_N, CROSS_S, EARLY_N, EARLY_S = range(15)
COPIES = 15
EAST, WEST, NORTH, SOUTH = 0, 1, 0, 1


def levels_loop(lower, upper, body, carry, times):
    whole = (upper - lower) // times

    def some(i, carry):
        for j in range(times):
            carry = body(lower + i * times + j, carry)
        return carry

    if whole > 0:
        carry = lax.fori_loop(0, whole, some, carry)
    for k in range(lower + whole * times, upper):
        carry = body(k, carry)
    return carry


def finished(value, pair, row_got, spot, slot):
    rows, cols = value.shape
    lane8 = lax.broadcasted_iota(jnp.int32, (8, cols), 1)
    row8 = lax.broadcasted_iota(jnp.int32, (8, cols), 0)
    ends8 = jnp.logical_or(lane8 == 0, lane8 == cols - 1)
    parts = []
    for r in range(0, rows, 8):
        turned = pltpu.roll(pair[r:r + 8], cols - 1 - 2 * spot, 1)
        total = value[r:r + 8] + jnp.where(ends8, turned, 0.0)
        if r == 0:
            total = total + jnp.where(row8 == 0, row_got[SOUTH, slot:slot + 1], 0.0)
        if r == rows - 8:
            total = total + jnp.where(row8 == 7, row_got[NORTH, slot:slot + 1], 0.0)
        parts.append(total)
    return jnp.concatenate(parts, axis=0)


def finish_kernel(value, pair, row_got, out_h, done, sems):
    _, fields, levels, rows, cols = value.shape
    half = fields // 2
    pairs = [pair[i] for i in range(half)]
    pieces = sems.shape[0] // fields
    span = levels // pieces
    copies = []
    for q in range(fields):
        for k in range(levels):
            slot = 2 * levels * (q % half) + 2 * k + q // half
            done[q, k] = finished(value[0, q, k], pairs[q // half], row_got, (q % half) * levels + k, slot)
            if (k + 1) % span == 0:
                part = pl.ds(k + 1 - span, span)
                copies.append(pltpu.make_async_copy(done.at[q, part], out_h.at[0, q, part], sems.at[len(copies)]))
                copies[-1].start()
    for copy in copies:
        copy.wait()


def kernel(
    lats, lons, adj_h, mask_h, depth_h, weight_h, diff_h, vel_h, mix_h,
    out_v, pair_v, row_got,
    field_a, field_b, diff, vel, mix, mask_i, depth, weight, mask_f,
    share, flux, col_depth, col_rate, col_coef, row_rate, row_coef, row_own, row_keep, row_corner, early_out, early_in,
    col_out, col_in, col_side_out, col_side_in, row_out, row_in, row_side_out, row_side_in,
    load_sem, send_sem, recv_sem,
):
    fields, levels, rows, cols = field_a.shape
    steps = diff.shape[0]
    half = fields // 2
    group = 2 * levels
    slots = fields * levels
    ice, lat, lon = lax.axis_index("ice"), lax.axis_index("lat"), lax.axis_index("lon")
    top, bottom = lat == lats - 1, lat == 0
    lon_e, lon_w = lax.rem(lon + 1, lons), lax.rem(lon + lons - 1, lons)
    lat_n = jnp.where(top, lat, lat + 1)
    lon_n = jnp.where(top, lons - 1 - lon, lon)
    lat_s = jnp.where(bottom, 0, lat - 1)
    partner = (1 - ice, lat, lon)
    east, west, north, south = [
        [(section, y, x) for section in (ice, 1 - ice)]
        for y, x in ((lat, lon_e), (lat, lon_w), (lat_n, lon_n), (lat_s, lon))
    ]

    barrier = pltpu.get_barrier_semaphore()
    for peer in [partner] + east + west + north:
        pl.semaphore_signal(barrier, inc=1, device_id=peer, device_id_type=MESH)

    @pl.when(jnp.logical_not(bottom))
    def _():
        for peer in south:
            pl.semaphore_signal(barrier, inc=1, device_id=peer, device_id_type=MESH)

    first = [
        pltpu.make_async_copy(depth_h.at[0], depth, load_sem.at[0]),
        pltpu.make_async_copy(weight_h.at[0], weight, load_sem.at[1]),
        pltpu.make_async_copy(mask_h, mask_i, load_sem.at[2]),
    ]
    coeffs = []
    for moment in range(steps - 1):
        base = 12 + 3 * moment
        coeffs.append([
            pltpu.make_async_copy(diff_h.at[moment, 0], diff.at[moment], load_sem.at[base]),
            pltpu.make_async_copy(vel_h.at[moment, 0], vel.at[moment], load_sem.at[base + 1]),
            pltpu.make_async_copy(mix_h.at[moment, 0], mix.at[moment], load_sem.at[base + 2]),
        ])
    moment = steps - 1
    last_mix = pltpu.make_async_copy(mix_h.at[moment, 0], mix.at[moment], load_sem.at[12 + 3 * moment])
    parts = []
    for i, (r, n) in enumerate(((rows - 8, 8), (0, 8), (8, rows - 16))):
        part = pl.ds(r, n)
        parts.append([
            pltpu.make_async_copy(adj_h.at[0, :, :, part], field_a.at[:, :, part], load_sem.at[3 + i]),
            pltpu.make_async_copy(diff_h.at[moment, 0, :, part], diff.at[moment, :, part], load_sem.at[6 + i]),
            pltpu.make_async_copy(vel_h.at[moment, 0, :, :, part], vel.at[moment, :, :, part], load_sem.at[9 + i]),
        ])
    for copies in [first] + parts + [[last_mix]] + coeffs[::-1]:
        for copy in copies:
            copy.start()

    lane = lax.broadcasted_iota(jnp.int32, (rows, cols), 1)
    row = lax.broadcasted_iota(jnp.int32, (rows, cols), 0)
    odd = (lane & 1) == 1
    low = lane < group
    used = lane < slots
    lane_level = jnp.where(low, lane, lane - group) >> 1
    lane8 = lax.broadcasted_iota(jnp.int32, (8, cols), 1)
    row8 = lax.broadcasted_iota(jnp.int32, (8, cols), 0)
    ends8 = jnp.logical_or(lane8 == 0, lane8 == cols - 1)
    slot_row = lax.broadcasted_iota(jnp.int32, (slots, cols), 0)
    slot_lane = lax.broadcasted_iota(jnp.int32, (slots, cols), 1)
    slot_level = jnp.where(slot_row < group, slot_row, slot_row - group) >> 1
    zero = jnp.zeros((rows, cols), jnp.float32)
    f32 = jnp.float32

    def slot_of(q, k):
        return group * (q % half) + 2 * k + q // half

    @pl.when(bottom)
    def _():
        row_in[:, SOUTH] = jnp.zeros_like(row_in[:, SOUTH])
        early_in[:, SOUTH] = jnp.zeros_like(early_in[:, SOUTH])
        row_side_in[:, :, SOUTH] = jnp.zeros_like(row_side_in[:, :, SOUTH])

    def remote(step, which, src, dst, peer):
        return pltpu.make_async_remote_copy(
            src_ref=src, dst_ref=dst, send_sem=send_sem.at[step, which],
            recv_sem=recv_sem.at[step, which], device_id=peer, device_id_type=MESH,
        )

    def col_copies(step):
        return [
            (remote(step, COL_E, col_out.at[step, EAST], col_in.at[step, WEST], east[0]), None),
            (remote(step, COL_W, col_out.at[step, WEST], col_in.at[step, EAST], west[0]), None),
        ]

    def row_pair(step, which_n, which_s, out, into, section):
        north_in, south_in = into(NORTH), into(SOUTH)
        peer_n, peer_s = north[section], south[section]
        return [
            (remote(step, which_n, out.at[step, NORTH], north_in, peer_n), top),
            (remote(step, which_s, out.at[step, NORTH], south_in, peer_n), jnp.logical_not(top)),
            (remote(step, which_n, out.at[step, SOUTH], north_in, peer_s), jnp.logical_not(bottom)),
        ]

    def row_copies():
        return row_pair(0, ROW_N, ROW_S, row_out, lambda side: row_in.at[0, side], 0)

    def early_copies():
        return row_pair(0, EARLY_N, EARLY_S, early_out, lambda side: early_in.at[0, side], 0)

    def side_copies(step):
        copies = []
        for section, names in enumerate(((SIDE_E, SIDE_W, SIDE_N, SIDE_S), (CROSS_E, CROSS_W, CROSS_N, CROSS_S))):
            for which, side, peer in ((names[0], EAST, east), (names[1], WEST, west)):
                copies.append((remote(
                    step, which, col_side_out.at[step, side], col_side_in.at[step, section, 1 - side], peer[section]
                ), None))
            copies += row_pair(
                step, names[2], names[3], row_side_out, lambda side: row_side_in.at[step, section, side], section
            )
        return copies

    def start(copies):
        for copy, go in copies:
            if go is None:
                copy.start()
            else:
                pl.when(go)(copy.start)

    def start_rows(copies):
        odd_lat = lax.rem(lat, 2) == 1
        even_lat = jnp.logical_not(odd_lat)
        start([(copy, jnp.logical_and(go, odd_lat)) for copy, go in copies[:2]])
        start(copies[2:])
        start([(copy, jnp.logical_and(go, even_lat)) for copy, go in copies[:2]])

    def wait_recv(copies):
        rest = []
        for copy, go in copies:
            if go is None:
                copy.wait_recv()
            else:
                rest.append(copy)
        for i in range(0, len(rest), 3):
            rest[i].wait_recv()
            pl.when(jnp.logical_not(bottom))(rest[i + 1].wait_recv)

    def pack(packed, q, k, value):
        slot, spot = q // half, (q % half) * levels + k
        turned = pltpu.roll(value, 2 * spot + 1, 1)
        packed = list(packed)
        packed[slot] = jnp.where((lane >> 1) == spot, turned, packed[slot])
        return tuple(packed)

    def gather(packed, src, lower, upper):
        for k in range(lower, upper):
            for q in range(fields):
                packed = pack(packed, q, k, src[q, k])
        return packed

    def split(packed):
        east_side = jnp.where(odd, pltpu.roll(packed[1], 1, 1), packed[0])
        west_side = jnp.where(odd, packed[1], pltpu.roll(packed[0], cols - 1, 1))
        return east_side, west_side

    def joined(from_west, from_east):
        first = jnp.where(odd, pltpu.roll(from_west, 1, 1), from_east)
        second = jnp.where(odd, from_west, pltpu.roll(from_east, cols - 1, 1))
        return first, second

    def take_row(src, side):
        flat = src.reshape(fields, levels * rows, cols)
        r = (rows - 1, 0)[side]
        for q in range(fields):
            row_own[side, pl.ds(slot_of(q, 0), levels, stride=2)] = flat[q, pl.ds(r, levels, stride=rows)]

    def row_local(moment, side, src):
        flat = src.reshape(fields, levels * rows, cols)
        diff_rows, mix_rows = diff.reshape(steps, levels * rows, cols), mix.reshape(steps, levels * rows, cols)
        vel_rows = vel.reshape(steps, 2, levels * rows, cols)
        r, inner, sign = ((rows - 1, rows - 2, -1.0), (0, 1, 1.0))[side]
        line, near = pl.ds(r, levels, stride=rows), pl.ds(inner, levels, stride=rows)
        level = lax.broadcasted_iota(jnp.int32, (levels, cols), 0)
        at = lax.broadcasted_iota(jnp.int32, (levels, cols), 1)
        m = mask_f[r:r + 1]
        d, z, v = diff_rows[moment, line] * m, vel_rows[moment, 0, line] * m, mix_rows[moment, line] * m
        own = m - 4.0 * d - 2.0 * v
        eastward = jnp.where(at == cols - 1, 0.0, d - z)
        westward = jnp.where(at == 0, 0.0, d + z)
        inward = (diff_rows[moment, near] + sign * vel_rows[moment, 1, near]) * mask_f[inner:inner + 1]
        for q in range(fields):
            a = flat[q, line]
            total = own * a + inward * flat[q, near]
            total = total + jnp.where(level == 0, 0.0, pltpu.roll(v * a, 1, 0))
            total = total + jnp.where(level == levels - 1, 0.0, pltpu.roll(v * a, levels - 1, 0))
            total = total + pltpu.roll(eastward * a, 1, 1) + pltpu.roll(westward * a, cols - 1, 1)
            row_own[side, pl.ds(slot_of(q, 0), levels, stride=2)] = total

    def row_coefs(moment, side):
        diff_rows, vel_rows = diff.reshape(steps, levels * rows, cols), vel.reshape(steps, 2, levels * rows, cols)
        r, sign = ((rows - 1, -1.0), (0, 1.0))[side]
        line = pl.ds(r, levels, stride=rows)
        value = (diff_rows[moment, line] + sign * vel_rows[moment, 1, line]) * mask_f[r:r + 1]
        for g in range(half):
            for p in range(2):
                row_coef[moment * 2 + side, pl.ds(g * group + p, levels, stride=2)] = value

    def col_coefs(moment):
        packed = zero
        for k in range(levels):
            d, z = diff[moment, k] * mask_f[...], vel[moment, 0, k] * mask_f[...]
            both = d + jnp.where(lane == cols - 1, -z, z)
            turned = pltpu.roll(both, 2 * k + 1, 1)
            packed = jnp.where((lane >> 1) == k, turned, packed)
        for side, value in (
            (EAST, jnp.where(odd, pltpu.roll(packed, 1, 1), packed)),
            (WEST, jnp.where(odd, packed, pltpu.roll(packed, cols - 1, 1))),
        ):
            col_coef[moment, side] = jnp.where(low, value, pltpu.roll(value, group, 1))

    def edge_rates():
        inverse = 1.0 / depth[...].astype(f32)
        for side, c in ((EAST, cols - 1), (WEST, 0)):
            rate = zero
            for q in range(fields):
                own = jnp.broadcast_to((weight[q] * inverse)[:, c:c + 1], (rows, cols))
                rate = jnp.where(lane == slot_of(q, 0), own, rate)
            col_rate[side] = rate
            col_depth[side] = jnp.broadcast_to(depth[:, c:c + 1], (rows, cols))
        for side, r in ((NORTH, rows - 1), (SOUTH, 0)):
            for g in range(half):
                rate = jnp.zeros((8, cols), f32)
                for p in range(2):
                    own = weight[g + p * half, r:r + 1] * inverse[r:r + 1]
                    rate = jnp.where(row8 == p, own, rate)
                row_rate[side, g] = rate

    def put_cols(step, moment, sides):
        for side, value in zip((EAST, WEST), sides):
            coef = col_coef[moment, side]
            col_out[step, side] = jnp.where(used, coef * value, pltpu.roll(coef, slots, 1))

    def put_row(moment, side, value):
        row_out[0, side, 0:slots] = row_coef[moment * 2 + side] * value
        row_out[0, side, slots:slots + 8] = row_coef[moment * 2 + side, 0:8]

    def put_early(moment, side, value):
        early_out[0, side, 0:slots] = row_coef[moment * 2 + side] * value
        early_out[0, side, slots:slots + group] = row_coef[moment * 2 + side, 0:group]

    def put_sides(step, col_sides, row_sides, ends=None):
        col_given = []
        for side, value in zip((EAST, WEST), col_sides):
            total = jnp.where(jnp.logical_and(used, lane_level < col_depth[side]), value, 0.0)
            turns = [pltpu.roll(total, cols - n, 1) for n in (2, 4, 6)]
            total = (total + turns[0]) + (turns[1] + turns[2])
            turns = [pltpu.roll(total, cols - n, 1) for n in (8, 16, 24, 32, 40)]
            total = ((total + turns[0]) + (turns[1] + turns[2])) + (turns[3] + turns[4])
            given = col_rate[side] * total
            col_given.append(given)
            out = given[0:8]
            for i in range(1, rows // 8):
                out = out + pltpu.roll(given[8 * i:8 * i + 8], 2 * i, 1)
            col_side_out[step, side] = out
        for side, value, r in zip((NORTH, SOUTH), row_sides, (rows - 1, 0)):
            live = jnp.where(slot_level < depth[r:r + 1], value, 0.0)
            out = jnp.zeros((8, cols), f32)
            for g in range(half):
                total = live[g * group:g * group + 8]
                for i in range(8, group, 8):
                    total = total + live[g * group + i:g * group + i + 8]
                total = (total + pltpu.roll(total, 2, 0)) + (pltpu.roll(total, 4, 0) + pltpu.roll(total, 6, 0))
                given = row_rate[side, g] * total
                out = out + (pltpu.roll(given, 2 * g, 0) if g else given)
            if ends is not None:
                for way, c in ((EAST, cols - 1), (WEST, 0)):
                    line = jnp.broadcast_to(col_given[way][r:r + 1], (8, cols))
                    for g in range(half):
                        for p in range(2):
                            shift = (c - group * g - p) % cols
                            turned = pltpu.roll(line, shift, 1) if shift else line
                            out = jnp.where(jnp.logical_and(row8 == 2 * g + p, lane8 == c), turned, out)
                    out = jnp.where(row8 == 4 + way, row_corner[side, way:way + 1] * ends[way][r:r + 1], out)
            row_side_out[step, side] = out

    def receive_cols(step):
        got = []
        for side in (EAST, WEST):
            value = col_in[step, side]
            coef = jnp.where(low, pltpu.roll(value, cols - slots, 1), pltpu.roll(value, cols - slots + group, 1))
            given = col_side_in[step, 1, side] - col_side_in[step, 0, side]
            given = jnp.concatenate(
                [given] + [pltpu.roll(given, cols - 2 * i, 1) for i in range(1, rows // 8)], axis=0
            )
            term = jnp.where(lane_level == 0, coef * given, 0.0)
            got.append(jnp.where(used, value + term, 0.0))
        return got

    def mirrored(value):
        at = lax.broadcasted_iota(jnp.int32, value.shape, 1)
        return jnp.take_along_axis(value, cols - 1 - at, axis=1)

    def receive_rows(main):
        for side in (NORTH, SOUTH):
            row_got[side] = main[0, side, 0:slots]

        @pl.when(top)
        def _():
            turned = mirrored(row_got[NORTH])
            row_got[NORTH] = jnp.where((slot_row & 1) == 1, -turned, turned)
            main[0, NORTH, slots:slots + 8] = mirrored(main[0, NORTH, slots:slots + 8])

    def receive_early():
        receive_rows(early_in)

        @pl.when(top)
        def _():
            block = slice(slots + 8, slots + group)
            early_in[0, NORTH, block] = mirrored(early_in[0, NORTH, block])

        for side in (NORTH, SOUTH):
            for g in range(half):
                block = slice(g * group, (g + 1) * group)
                more = early_in[0, side, slots:slots + group] * row_keep[side, block]
                row_got[side, block] = row_got[side, block] + more

    def add_shares(step, main):
        for side in (NORTH, SOUTH):
            given = row_side_in[step, 1, side] - row_side_in[step, 0, side]
            if side == NORTH:
                turned = mirrored(given)
                given = jnp.where(top, jnp.where((row8 & 1) == 1, -turned, turned), given)
            coef = main[0, side, slots:slots + 1]
            for g in range(half):
                block = slice(g * group, g * group + 8)
                term = pltpu.roll(given, 8 - 2 * g, 0) if g else given
                row_got[side, block] = row_got[side, block] + jnp.where(row8 < 2, coef * term, 0.0)

    def receive_late(step, got):
        add_shares(step, early_in)
        lines = [[row_side_in[step, 0, side, 4 + way:5 + way] for way in (EAST, WEST)] for side in (NORTH, SOUTH)]
        folded = [jnp.where(odd[0:1], -line, line) for line in lines[NORTH][::-1]]
        out = []
        for way, value in zip((EAST, WEST), got):
            line = jnp.where(top, folded[way], lines[NORTH][way])
            value = value + jnp.where(row == rows - 1, line, 0.0)
            out.append(value + jnp.where(row == 0, lines[SOUTH][way], 0.0))
        return out

    def col_corner(value):
        out = []
        for c in (cols - 1, 0):
            whole = jnp.broadcast_to(value[:, c:c + 1], (slots, cols))
            whole = jnp.where(slot_lane == slot_row, whole, 0.0)
            out.append(jnp.sum(whole, axis=0, keepdims=True))
        return out

    def interior(moment, k, src, dst, first=False, last=False):
        mask = mask_f[...]
        d, z, b = diff[moment, k] * mask, vel[moment, 0, k] * mask, vel[moment, 1, k] * mask
        own = mask - 4.0 * d - 2.0 * (mix[moment, k] * mask)
        above = None if first else mix[moment, k - 1] * mask
        below = None if last else mix[moment, k + 1] * mask
        eastward = jnp.where(lane == cols - 1, 0.0, d - z)
        westward = jnp.where(lane == 0, 0.0, d + z)
        northward = jnp.where(row == rows - 1, 0.0, d - b)
        southward = jnp.where(row == 0, 0.0, d + b)
        for q in range(fields):
            a = src[q, k]
            total = own * a
            if not first:
                total = total + above * src[q, k - 1]
            if not last:
                total = total + below * src[q, k + 1]
            total = total + pltpu.roll(eastward * a, 1, 1) + pltpu.roll(westward * a, cols - 1, 1)
            total = total + pltpu.roll(northward * a, 1, 0) + pltpu.roll(southward * a, rows - 1, 0)
            dst[q, k] = total

    for copy in first:
        copy.wait()
    mask_f[...] = mask_i[...].astype(f32)
    edge_rates()
    for side in (NORTH, SOUTH):
        for copy in parts[side]:
            copy.wait()
        take_row(field_a, side)
        row_coefs(steps - 1, side)
        put_row(steps - 1, side, row_own[side])

    @pl.when(bottom)
    def _():
        pl.semaphore_wait(barrier, 7)

    @pl.when(jnp.logical_not(bottom))
    def _():
        pl.semaphore_wait(barrier, 9)

    row_halo = row_copies()
    start_rows(row_halo)
    for copy in parts[2]:
        copy.wait()
    own_cols = split(gather((zero, zero), field_a, 0, levels))
    col_coefs(steps - 1)
    put_cols(0, steps - 1, own_cols)
    col_halo = col_copies(0)
    start(col_halo)
    put_sides(0, own_cols, (row_own[NORTH], row_own[SOUTH]))
    side_halo = side_copies(0)
    start(side_halo)
    late = col_halo + side_halo
    pending = row_halo + late

    def add(k, sums):
        live = k < depth[...]
        return tuple(s + jnp.where(live, field_a[q, k], 0.0) for q, s in enumerate(sums))

    sums = levels_loop(0, levels, add, (zero,) * fields, SUM)
    last_mix.wait()

    for step in range(steps):
        moment = steps - 1 - step
        src, dst = (field_a, field_b) if step % 2 == 0 else (field_b, field_a)
        final = step == steps - 1
        if final:
            dst = out_v.at[0]
        scale = 1.0 / depth[...].astype(f32)
        for q in range(fields):
            share[step, q] = weight[q] * (scale * sums[q])
        couple = remote(step, COUPLE, share.at[step], flux.at[step], partner)
        couple.start()
        pending = pending + [(couple, None)]

        def inner(k, carry, **ends):
            interior(moment, k, src, dst, **ends)
            return carry

        split_at = levels - 1 if final else 2 + 2 * INNER
        levels_loop(2, split_at, inner, 0, INNER)
        if final:
            inner(levels - 1, 0, last=True)
        couple.wait_recv()
        for q in range(fields):
            src[q, 0] = src[q, 0] + (flux[step, q] - share[step, q])
        if not final:
            for copy in coeffs[moment - 1]:
                copy.wait()
            for side in (NORTH, SOUTH):
                row_local(moment, side, src)
                row_coefs(moment - 1, side)
                put_early(moment - 1, side, row_own[side])
            early = early_copies()
            start_rows(early)
            levels_loop(split_at, levels - 1, inner, 0, INNER)
            inner(levels - 1, 0, last=True)
        inner(0, 0, first=True)
        inner(1, 0)
        if not final:
            own_e, own_w = split(gather((zero, zero), dst, 0, levels))
            col_coefs(moment - 1)
            for side, r in ((NORTH, rows - 1), (SOUTH, 0)):
                for way, line in enumerate(col_corner(row_coef[2 * (moment - 1) + side])):
                    row_corner[side, way:way + 1] = line
                row_keep[side] = row_out[0, side, 0:slots]
                for q in range(fields):
                    at = slice(slot_of(q, 0), slot_of(q, 0) + 1)
                    row_keep[side, at] = row_coef[2 * moment + side, at] * src[q, 0, r:r + 1]

        wait_recv(early if final else row_halo)
        if final:
            receive_early()
        else:
            receive_rows(row_in)
        wait_recv(late)
        got_e, got_w = receive_cols(step)
        if final:
            got_e, got_w = receive_late(step, (got_e, got_w))
        else:
            add_shares(step, row_in)
            col_more = [col_corner(row_got[side]) for side in (NORTH, SOUTH)]
            col_sides = []
            for side, value in ((EAST, own_e + got_e), (WEST, own_w + got_w)):
                value = value + jnp.where(row == rows - 1, col_more[NORTH][side], 0.0)
                col_sides.append(value + jnp.where(row == 0, col_more[SOUTH][side], 0.0))
            put_cols(step + 1, moment - 1, col_sides)
            col_halo = col_copies(step + 1)
            start(col_halo)
            row_sides = [row_own[side] + row_got[side] for side in (NORTH, SOUTH)]
            put_sides(step + 1, col_sides, row_sides, (got_e, got_w))
            side_halo = side_copies(step + 1)
            start(side_halo)
            late = col_halo + side_halo
            pending = pending + early + late

        pair = joined(got_w, got_e)
        if final:
            pair_v[0], pair_v[1] = pair
            break

        sums = [zero] * fields
        for k in range(levels):
            for q in range(fields):
                total = finished(dst[q, k], pair[q // half], row_got, (q % half) * levels + k, slot_of(q, k))
                dst[q, k] = total
                sums[q] = sums[q] + jnp.where(k < depth[...], total, 0.0)

    for copy, go in pending:
        if go is None:
            copy.wait_send()
        else:
            pl.when(go)(copy.wait_send)


def solution(mesh):
    lats, lons = mesh.shape["lat"], mesh.shape["lon"]

    def shards(adjoint, land_mask, coupling_depth, coupling_weight, diffusion, velocity, mixing):
        _, fields, levels, rows, cols = adjoint.shape
        steps = diffusion.shape[0]
        f32 = jnp.float32
        block = (rows, cols)
        slots = fields * levels
        column = pltpu.VMEM((steps, 2, rows, cols), f32)
        edge = pltpu.VMEM((1, 2, slots + 8, cols), f32)
        early = pltpu.VMEM((1, 2, slots + 2 * levels, cols), f32)
        side_out, side_in = pltpu.VMEM((steps, 2, 8, cols), f32), pltpu.VMEM((steps, 2, 2, 8, cols), f32)
        parts = pl.pallas_call(
            functools.partial(kernel, lats, lons),
            out_shape=(
                jax.ShapeDtypeStruct(adjoint.shape, f32),
                jax.ShapeDtypeStruct((2, rows, cols), f32),
                jax.ShapeDtypeStruct((2, slots, cols), f32),
            ),
            in_specs=[pl.BlockSpec(memory_space=pltpu.HBM)] * 7,
            out_specs=(pl.BlockSpec(memory_space=pltpu.VMEM),) * 3,
            scratch_shapes=[
                pltpu.VMEM((fields, levels, rows, cols), f32),
                pltpu.VMEM((fields, levels, rows, cols), f32),
                pltpu.VMEM((steps, levels, rows, cols), f32),
                pltpu.VMEM((steps, 2, levels, rows, cols), f32),
                pltpu.VMEM((steps, levels, rows, cols), f32),
                pltpu.VMEM(block, jnp.int32),
                pltpu.VMEM(block, jnp.int32),
                pltpu.VMEM((fields, rows, cols), f32),
                pltpu.VMEM(block, f32),
                pltpu.VMEM((steps, fields, rows, cols), f32),
                pltpu.VMEM((steps, fields, rows, cols), f32),
                pltpu.VMEM((2, rows, cols), jnp.int32),
                pltpu.VMEM((2, rows, cols), f32),
                column,
                pltpu.VMEM((2, fields // 2, 8, cols), f32),
                pltpu.VMEM((steps * 2, slots, cols), f32),
                pltpu.VMEM((2, slots, cols), f32),
                pltpu.VMEM((2, slots, cols), f32),
                pltpu.VMEM((2, 8, cols), f32),
                early, early,
                column, column, side_out, side_in,
                edge, edge, side_out, side_in,
                pltpu.SemaphoreType.DMA((10 + 3 * steps,)),
                pltpu.SemaphoreType.DMA((steps, COPIES)),
                pltpu.SemaphoreType.DMA((steps, COPIES)),
            ],
            compiler_params=pltpu.CompilerParams(
                collective_id=0, has_side_effects=True, vmem_limit_bytes=40 * 1024 * 1024
            ),
            name="adjoint",
        )(*(pltpu.with_memory_space_constraint(x, pltpu.HBM) for x in (adjoint, land_mask, coupling_depth, coupling_weight, diffusion, velocity, mixing)))
        return pl.pallas_call(
            finish_kernel,
            out_shape=jax.ShapeDtypeStruct(adjoint.shape, f32),
            in_specs=[pl.BlockSpec(memory_space=pltpu.VMEM)] * 3,
            out_specs=pl.BlockSpec(memory_space=pltpu.HBM),
            scratch_shapes=[
                pltpu.VMEM((fields, levels, rows, cols), f32), pltpu.SemaphoreType.DMA((PIECES * fields,)),
            ],
            compiler_params=pltpu.CompilerParams(vmem_limit_bytes=16 * 1024 * 1024),
            name="adjoint_finish",
        )(*parts)

    in_specs = (
        P("ice", None, None, "lat", "lon"),
        P("lat", "lon"),
        P("ice", "lat", "lon"),
        P("ice", None, "lat", "lon"),
        P(None, "ice", None, "lat", "lon"),
        P(None, "ice", None, None, "lat", "lon"),
        P(None, "ice", None, "lat", "lon"),
    )
    out_specs = P("ice", None, None, "lat", "lon")
    return jax.shard_map(shards, mesh=mesh, in_specs=in_specs, out_specs=out_specs, check_vma=False)
```

```python
import functools

import jax
import jax.numpy as jnp
from jax import lax
from jax.experimental import pallas as pl
from jax.experimental.pallas import tpu as pltpu
from jax.sharding import PartitionSpec as P

MESH = pl.DeviceIdType.MESH
INNER, SUM, PIECES = 7, 4, 2
COUPLE, COL_E, COL_W, ROW_N, ROW_S, SIDE_E, SIDE_W, SIDE_N, SIDE_S, CROSS_E, CROSS_W, CROSS_N, CROSS_S, EARLY_N, EARLY_S = range(15)
COPIES = 15
EAST, WEST, NORTH, SOUTH = 0, 1, 0, 1


def levels_loop(lower, upper, body, carry, times):
    whole = (upper - lower) // times

    def some(i, carry):
        for j in range(times):
            carry = body(lower + i * times + j, carry)
        return carry

    if whole > 0:
        carry = lax.fori_loop(0, whole, some, carry)
    for k in range(lower + whole * times, upper):
        carry = body(k, carry)
    return carry


def finished(value, pair, row_got, spot, slot):
    rows, cols = value.shape
    lane8 = lax.broadcasted_iota(jnp.int32, (8, cols), 1)
    row8 = lax.broadcasted_iota(jnp.int32, (8, cols), 0)
    ends8 = jnp.logical_or(lane8 == 0, lane8 == cols - 1)
    parts = []
    for r in range(0, rows, 8):
        turned = pltpu.roll(pair[r:r + 8], cols - 1 - 2 * spot, 1)
        total = value[r:r + 8] + jnp.where(ends8, turned, 0.0)
        if r == 0:
            total = total + jnp.where(row8 == 0, row_got[SOUTH, slot:slot + 1], 0.0)
        if r == rows - 8:
            total = total + jnp.where(row8 == 7, row_got[NORTH, slot:slot + 1], 0.0)
        parts.append(total)
    return jnp.concatenate(parts, axis=0)


def finish_kernel(value, pair, row_got, out_h, done, sems):
    _, fields, levels, rows, cols = value.shape
    half = fields // 2
    pairs = [pair[i] for i in range(half)]
    pieces = sems.shape[0] // fields
    span = levels // pieces
    copies = []
    for q in range(fields):
        for k in range(levels):
            slot = 2 * levels * (q % half) + 2 * k + q // half
            done[q, k] = finished(value[0, q, k], pairs[q // half], row_got, (q % half) * levels + k, slot)
            if (k + 1) % span == 0:
                part = pl.ds(k + 1 - span, span)
                copies.append(pltpu.make_async_copy(done.at[q, part], out_h.at[0, q, part], sems.at[len(copies)]))
                copies[-1].start()
    for copy in copies:
        copy.wait()


def kernel(
    lats, lons, adj_h, mask_h, depth_h, weight_h, diff_h, vel_h, mix_h,
    out_v, pair_v, row_got,
    field_a, field_b, diff, vel, mix, mask_i, depth, weight, mask_f,
    share, flux, col_depth, col_rate, col_coef, row_rate, row_coef, row_own, row_keep, row_corner, early_out, early_in,
    col_out, col_in, col_side_out, col_side_in, row_out, row_in, row_side_out, row_side_in,
    load_sem, send_sem, recv_sem,
):
    fields, levels, rows, cols = field_a.shape
    steps = diff.shape[0]
    half = fields // 2
    group = 2 * levels
    slots = fields * levels
    ice, lat, lon = lax.axis_index("ice"), lax.axis_index("lat"), lax.axis_index("lon")
    top, bottom = lat == lats - 1, lat == 0
    lon_e, lon_w = lax.rem(lon + 1, lons), lax.rem(lon + lons - 1, lons)
    lat_n = jnp.where(top, lat, lat + 1)
    lon_n = jnp.where(top, lons - 1 - lon, lon)
    lat_s = jnp.where(bottom, 0, lat - 1)
    partner = (1 - ice, lat, lon)
    east, west, north, south = [
        [(section, y, x) for section in (ice, 1 - ice)]
        for y, x in ((lat, lon_e), (lat, lon_w), (lat_n, lon_n), (lat_s, lon))
    ]

    barrier = pltpu.get_barrier_semaphore()
    for peer in [partner] + east + west + north:
        pl.semaphore_signal(barrier, inc=1, device_id=peer, device_id_type=MESH)

    @pl.when(jnp.logical_not(bottom))
    def _():
        for peer in south:
            pl.semaphore_signal(barrier, inc=1, device_id=peer, device_id_type=MESH)

    first = [
        pltpu.make_async_copy(depth_h.at[0], depth, load_sem.at[0]),
        pltpu.make_async_copy(weight_h.at[0], weight, load_sem.at[1]),
        pltpu.make_async_copy(mask_h, mask_i, load_sem.at[2]),
    ]
    coeffs = []
    for moment in range(steps - 1):
        base = 12 + 3 * moment
        coeffs.append([
            pltpu.make_async_copy(diff_h.at[moment, 0], diff.at[moment], load_sem.at[base]),
            pltpu.make_async_copy(vel_h.at[moment, 0], vel.at[moment], load_sem.at[base + 1]),
            pltpu.make_async_copy(mix_h.at[moment, 0], mix.at[moment], load_sem.at[base + 2]),
        ])
    moment = steps - 1
    last_mix = pltpu.make_async_copy(mix_h.at[moment, 0], mix.at[moment], load_sem.at[12 + 3 * moment])
    parts = []
    for i, (r, n) in enumerate(((rows - 8, 8), (0, 8), (8, rows - 16))):
        part = pl.ds(r, n)
        parts.append([
            pltpu.make_async_copy(adj_h.at[0, :, :, part], field_a.at[:, :, part], load_sem.at[3 + i]),
            pltpu.make_async_copy(diff_h.at[moment, 0, :, part], diff.at[moment, :, part], load_sem.at[6 + i]),
            pltpu.make_async_copy(vel_h.at[moment, 0, :, :, part], vel.at[moment, :, :, part], load_sem.at[9 + i]),
        ])
    for copies in [first] + parts + [[last_mix]] + coeffs[::-1]:
        for copy in copies:
            copy.start()

    lane = lax.broadcasted_iota(jnp.int32, (rows, cols), 1)
    row = lax.broadcasted_iota(jnp.int32, (rows, cols), 0)
    odd = (lane & 1) == 1
    low = lane < group
    used = lane < slots
    lane_level = jnp.where(low, lane, lane - group) >> 1
    lane8 = lax.broadcasted_iota(jnp.int32, (8, cols), 1)
    row8 = lax.broadcasted_iota(jnp.int32, (8, cols), 0)
    ends8 = jnp.logical_or(lane8 == 0, lane8 == cols - 1)
    slot_row = lax.broadcasted_iota(jnp.int32, (slots, cols), 0)
    slot_lane = lax.broadcasted_iota(jnp.int32, (slots, cols), 1)
    slot_level = jnp.where(slot_row < group, slot_row, slot_row - group) >> 1
    zero = jnp.zeros((rows, cols), jnp.float32)
    f32 = jnp.float32

    def slot_of(q, k):
        return group * (q % half) + 2 * k + q // half

    @pl.when(bottom)
    def _():
        row_in[:, SOUTH] = jnp.zeros_like(row_in[:, SOUTH])
        early_in[:, SOUTH] = jnp.zeros_like(early_in[:, SOUTH])
        row_side_in[:, :, SOUTH] = jnp.zeros_like(row_side_in[:, :, SOUTH])

    def remote(step, which, src, dst, peer):
        return pltpu.make_async_remote_copy(
            src_ref=src, dst_ref=dst, send_sem=send_sem.at[step, which],
            recv_sem=recv_sem.at[step, which], device_id=peer, device_id_type=MESH,
        )

    def col_copies(step):
        return [
            (remote(step, COL_E, col_out.at[step, EAST], col_in.at[step, WEST], east[0]), None),
            (remote(step, COL_W, col_out.at[step, WEST], col_in.at[step, EAST], west[0]), None),
        ]

    def row_pair(step, which_n, which_s, out, into, section):
        north_in, south_in = into(NORTH), into(SOUTH)
        peer_n, peer_s = north[section], south[section]
        return [
            (remote(step, which_n, out.at[step, NORTH], north_in, peer_n), top),
            (remote(step, which_s, out.at[step, NORTH], south_in, peer_n), jnp.logical_not(top)),
            (remote(step, which_n, out.at[step, SOUTH], north_in, peer_s), jnp.logical_not(bottom)),
        ]

    def row_copies():
        return row_pair(0, ROW_N, ROW_S, row_out, lambda side: row_in.at[0, side], 0)

    def early_copies():
        return row_pair(0, EARLY_N, EARLY_S, early_out, lambda side: early_in.at[0, side], 0)

    def side_copies(step):
        copies = []
        for section, names in enumerate(((SIDE_E, SIDE_W, SIDE_N, SIDE_S), (CROSS_E, CROSS_W, CROSS_N, CROSS_S))):
            for which, side, peer in ((names[0], EAST, east), (names[1], WEST, west)):
                copies.append((remote(
                    step, which, col_side_out.at[step, side], col_side_in.at[step, section, 1 - side], peer[section]
                ), None))
            copies += row_pair(
                step, names[2], names[3], row_side_out, lambda side: row_side_in.at[step, section, side], section
            )
        return copies

    def start(copies):
        for copy, go in copies:
            if go is None:
                copy.start()
            else:
                pl.when(go)(copy.start)

    def start_rows(copies):
        odd_lat = lax.rem(lat, 2) == 1
        even_lat = jnp.logical_not(odd_lat)
        start([(copy, jnp.logical_and(go, odd_lat)) for copy, go in copies[:2]])
        start(copies[2:])
        start([(copy, jnp.logical_and(go, even_lat)) for copy, go in copies[:2]])

    def wait_recv(copies):
        rest = []
        for copy, go in copies:
            if go is None:
                copy.wait_recv()
            else:
                rest.append(copy)
        for i in range(0, len(rest), 3):
            rest[i].wait_recv()
            pl.when(jnp.logical_not(bottom))(rest[i + 1].wait_recv)

    def pack(packed, q, k, value):
        slot, spot = q // half, (q % half) * levels + k
        turned = pltpu.roll(value, 2 * spot + 1, 1)
        packed = list(packed)
        packed[slot] = jnp.where((lane >> 1) == spot, turned, packed[slot])
        return tuple(packed)

    def gather(packed, src, lower, upper):
        for k in range(lower, upper):
            for q in range(fields):
                packed = pack(packed, q, k, src[q, k])
        return packed

    def split(packed):
        east_side = jnp.where(odd, pltpu.roll(packed[1], 1, 1), packed[0])
        west_side = jnp.where(odd, packed[1], pltpu.roll(packed[0], cols - 1, 1))
        return east_side, west_side

    def joined(from_west, from_east):
        first = jnp.where(odd, pltpu.roll(from_west, 1, 1), from_east)
        second = jnp.where(odd, from_west, pltpu.roll(from_east, cols - 1, 1))
        return first, second

    def take_row(src, side):
        flat = src.reshape(fields, levels * rows, cols)
        r = (rows - 1, 0)[side]
        for q in range(fields):
            row_own[side, pl.ds(slot_of(q, 0), levels, stride=2)] = flat[q, pl.ds(r, levels, stride=rows)]

    def row_local(moment, side, src):
        flat = src.reshape(fields, levels * rows, cols)
        diff_rows, mix_rows = diff.reshape(steps, levels * rows, cols), mix.reshape(steps, levels * rows, cols)
        vel_rows = vel.reshape(steps, 2, levels * rows, cols)
        r, inner, sign = ((rows - 1, rows - 2, -1.0), (0, 1, 1.0))[side]
        line, near = pl.ds(r, levels, stride=rows), pl.ds(inner, levels, stride=rows)
        level = lax.broadcasted_iota(jnp.int32, (levels, cols), 0)
        at = lax.broadcasted_iota(jnp.int32, (levels, cols), 1)
        m = mask_f[r:r + 1]
        d, z, v = diff_rows[moment, line] * m, vel_rows[moment, 0, line] * m, mix_rows[moment, line] * m
        own = m - 4.0 * d - 2.0 * v
        eastward = jnp.where(at == cols - 1, 0.0, d - z)
        westward = jnp.where(at == 0, 0.0, d + z)
        inward = (diff_rows[moment, near] + sign * vel_rows[moment, 1, near]) * mask_f[inner:inner + 1]
        for q in range(fields):
            a = flat[q, line]
            total = own * a + inward * flat[q, near]
            total = total + jnp.where(level == 0, 0.0, pltpu.roll(v * a, 1, 0))
            total = total + jnp.where(level == levels - 1, 0.0, pltpu.roll(v * a, levels - 1, 0))
            total = total + pltpu.roll(eastward * a, 1, 1) + pltpu.roll(westward * a, cols - 1, 1)
            row_own[side, pl.ds(slot_of(q, 0), levels, stride=2)] = total

    def row_coefs(moment, side):
        diff_rows, vel_rows = diff.reshape(steps, levels * rows, cols), vel.reshape(steps, 2, levels * rows, cols)
        r, sign = ((rows - 1, -1.0), (0, 1.0))[side]
        line = pl.ds(r, levels, stride=rows)
        value = (diff_rows[moment, line] + sign * vel_rows[moment, 1, line]) * mask_f[r:r + 1]
        for g in range(half):
            for p in range(2):
                row_coef[moment * 2 + side, pl.ds(g * group + p, levels, stride=2)] = value

    def col_coefs(moment):
        packed = zero
        for k in range(levels):
            d, z = diff[moment, k] * mask_f[...], vel[moment, 0, k] * mask_f[...]
            both = d + jnp.where(lane == cols - 1, -z, z)
            turned = pltpu.roll(both, 2 * k + 1, 1)
            packed = jnp.where((lane >> 1) == k, turned, packed)
        for side, value in (
            (EAST, jnp.where(odd, pltpu.roll(packed, 1, 1), packed)),
            (WEST, jnp.where(odd, packed, pltpu.roll(packed, cols - 1, 1))),
        ):
            col_coef[moment, side] = jnp.where(low, value, pltpu.roll(value, group, 1))

    def edge_rates():
        inverse = 1.0 / depth[...].astype(f32)
        for side, c in ((EAST, cols - 1), (WEST, 0)):
            rate = zero
            for q in range(fields):
                own = jnp.broadcast_to((weight[q] * inverse)[:, c:c + 1], (rows, cols))
                rate = jnp.where(lane == slot_of(q, 0), own, rate)
            col_rate[side] = rate
            col_depth[side] = jnp.broadcast_to(depth[:, c:c + 1], (rows, cols))
        for side, r in ((NORTH, rows - 1), (SOUTH, 0)):
            for g in range(half):
                rate = jnp.zeros((8, cols), f32)
                for p in range(2):
                    own = weight[g + p * half, r:r + 1] * inverse[r:r + 1]
                    rate = jnp.where(row8 == p, own, rate)
                row_rate[side, g] = rate

    def put_cols(step, moment, sides):
        for side, value in zip((EAST, WEST), sides):
            coef = col_coef[moment, side]
            col_out[step, side] = jnp.where(used, coef * value, pltpu.roll(coef, slots, 1))

    def put_row(moment, side, value):
        row_out[0, side, 0:slots] = row_coef[moment * 2 + side] * value
        row_out[0, side, slots:slots + 8] = row_coef[moment * 2 + side, 0:8]

    def put_early(moment, side, value):
        early_out[0, side, 0:slots] = row_coef[moment * 2 + side] * value
        early_out[0, side, slots:slots + group] = row_coef[moment * 2 + side, 0:group]

    def put_sides(step, col_sides, row_sides, ends=None):
        col_given = []
        for side, value in zip((EAST, WEST), col_sides or ()):
            total = jnp.where(jnp.logical_and(used, lane_level < col_depth[side]), value, 0.0)
            turns = [pltpu.roll(total, cols - n, 1) for n in (2, 4, 6)]
            total = (total + turns[0]) + (turns[1] + turns[2])
            turns = [pltpu.roll(total, cols - n, 1) for n in (8, 16, 24, 32, 40)]
            total = ((total + turns[0]) + (turns[1] + turns[2])) + (turns[3] + turns[4])
            given = col_rate[side] * total
            col_given.append(given)
            out = given[0:8]
            for i in range(1, rows // 8):
                out = out + pltpu.roll(given[8 * i:8 * i + 8], 2 * i, 1)
            col_side_out[step, side] = out
        for side, value, r in zip((NORTH, SOUTH), row_sides or (), (rows - 1, 0)):
            live = jnp.where(slot_level < depth[r:r + 1], value, 0.0)
            out = jnp.zeros((8, cols), f32)
            for g in range(half):
                total = live[g * group:g * group + 8]
                for i in range(8, group, 8):
                    total = total + live[g * group + i:g * group + i + 8]
                total = (total + pltpu.roll(total, 2, 0)) + (pltpu.roll(total, 4, 0) + pltpu.roll(total, 6, 0))
                given = row_rate[side, g] * total
                out = out + (pltpu.roll(given, 2 * g, 0) if g else given)
            if ends is not None:
                for way, c in ((EAST, cols - 1), (WEST, 0)):
                    line = jnp.broadcast_to(col_given[way][r:r + 1], (8, cols))
                    for g in range(half):
                        for p in range(2):
                            shift = (c - group * g - p) % cols
                            turned = pltpu.roll(line, shift, 1) if shift else line
                            out = jnp.where(jnp.logical_and(row8 == 2 * g + p, lane8 == c), turned, out)
                    out = jnp.where(row8 == 4 + way, row_corner[side, way:way + 1] * ends[way][r:r + 1], out)
            row_side_out[step, side] = out

    def receive_cols(step):
        got = []
        for side in (EAST, WEST):
            value = col_in[step, side]
            coef = jnp.where(low, pltpu.roll(value, cols - slots, 1), pltpu.roll(value, cols - slots + group, 1))
            given = col_side_in[step, 1, side] - col_side_in[step, 0, side]
            given = jnp.concatenate(
                [given] + [pltpu.roll(given, cols - 2 * i, 1) for i in range(1, rows // 8)], axis=0
            )
            term = jnp.where(lane_level == 0, coef * given, 0.0)
            got.append(jnp.where(used, value + term, 0.0))
        return got

    def mirrored(value):
        at = lax.broadcasted_iota(jnp.int32, value.shape, 1)
        return jnp.take_along_axis(value, cols - 1 - at, axis=1)

    def receive_rows(main):
        for side in (NORTH, SOUTH):
            row_got[side] = main[0, side, 0:slots]

        @pl.when(top)
        def _():
            turned = mirrored(row_got[NORTH])
            row_got[NORTH] = jnp.where((slot_row & 1) == 1, -turned, turned)
            main[0, NORTH, slots:slots + 8] = mirrored(main[0, NORTH, slots:slots + 8])

    def receive_early():
        receive_rows(early_in)

        @pl.when(top)
        def _():
            block = slice(slots + 8, slots + group)
            early_in[0, NORTH, block] = mirrored(early_in[0, NORTH, block])

        for side in (NORTH, SOUTH):
            for g in range(half):
                block = slice(g * group, (g + 1) * group)
                more = early_in[0, side, slots:slots + group] * row_keep[side, block]
                row_got[side, block] = row_got[side, block] + more

    def add_shares(step, main):
        for side in (NORTH, SOUTH):
            given = row_side_in[step, 1, side] - row_side_in[step, 0, side]
            if side == NORTH:
                turned = mirrored(given)
                given = jnp.where(top, jnp.where((row8 & 1) == 1, -turned, turned), given)
            coef = main[0, side, slots:slots + 1]
            for g in range(half):
                block = slice(g * group, g * group + 8)
                term = pltpu.roll(given, 8 - 2 * g, 0) if g else given
                row_got[side, block] = row_got[side, block] + jnp.where(row8 < 2, coef * term, 0.0)

    def receive_late(step, got):
        add_shares(step, early_in)
        lines = [[row_side_in[step, 0, side, 4 + way:5 + way] for way in (EAST, WEST)] for side in (NORTH, SOUTH)]
        folded = [jnp.where(odd[0:1], -line, line) for line in lines[NORTH][::-1]]
        out = []
        for way, value in zip((EAST, WEST), got):
            line = jnp.where(top, folded[way], lines[NORTH][way])
            value = value + jnp.where(row == rows - 1, line, 0.0)
            out.append(value + jnp.where(row == 0, lines[SOUTH][way], 0.0))
        return out

    def col_corner(value):
        out = []
        for c in (cols - 1, 0):
            whole = jnp.broadcast_to(value[:, c:c + 1], (slots, cols))
            whole = jnp.where(slot_lane == slot_row, whole, 0.0)
            out.append(jnp.sum(whole, axis=0, keepdims=True))
        return out

    def interior(moment, k, src, dst, first=False, last=False):
        mask = mask_f[...]
        d, z, b = diff[moment, k] * mask, vel[moment, 0, k] * mask, vel[moment, 1, k] * mask
        own = mask - 4.0 * d - 2.0 * (mix[moment, k] * mask)
        above = None if first else mix[moment, k - 1] * mask
        below = None if last else mix[moment, k + 1] * mask
        eastward = jnp.where(lane == cols - 1, 0.0, d - z)
        westward = jnp.where(lane == 0, 0.0, d + z)
        northward = jnp.where(row == rows - 1, 0.0, d - b)
        southward = jnp.where(row == 0, 0.0, d + b)
        for q in range(fields):
            a = src[q, k]
            total = own * a
            if not first:
                total = total + above * src[q, k - 1]
            if not last:
                total = total + below * src[q, k + 1]
            total = total + pltpu.roll(eastward * a, 1, 1) + pltpu.roll(westward * a, cols - 1, 1)
            total = total + pltpu.roll(northward * a, 1, 0) + pltpu.roll(southward * a, rows - 1, 0)
            dst[q, k] = total

    for copy in first:
        copy.wait()
    mask_f[...] = mask_i[...].astype(f32)
    edge_rates()
    for side in (NORTH, SOUTH):
        for copy in parts[side]:
            copy.wait()
        take_row(field_a, side)
        row_coefs(steps - 1, side)
        put_row(steps - 1, side, row_own[side])

    put_sides(0, None, (row_own[NORTH], row_own[SOUTH]))

    @pl.when(bottom)
    def _():
        pl.semaphore_wait(barrier, 7)

    @pl.when(jnp.logical_not(bottom))
    def _():
        pl.semaphore_wait(barrier, 9)

    row_halo = row_copies()
    start_rows(row_halo)
    side_halo = side_copies(0)
    start(side_halo[2:5] + side_halo[7:10])
    for copy in parts[2]:
        copy.wait()
    own_cols = split(gather((zero, zero), field_a, 0, levels))
    col_coefs(steps - 1)
    put_cols(0, steps - 1, own_cols)
    col_halo = col_copies(0)
    start(col_halo)
    put_sides(0, own_cols, None)
    start(side_halo[0:2] + side_halo[5:7])
    late = col_halo + side_halo
    pending = row_halo + late

    def add(k, sums):
        live = k < depth[...]
        return tuple(s + jnp.where(live, field_a[q, k], 0.0) for q, s in enumerate(sums))

    sums = levels_loop(0, levels, add, (zero,) * fields, SUM)
    last_mix.wait()

    for step in range(steps):
        moment = steps - 1 - step
        src, dst = (field_a, field_b) if step % 2 == 0 else (field_b, field_a)
        final = step == steps - 1
        if final:
            dst = out_v.at[0]
        scale = 1.0 / depth[...].astype(f32)
        for q in range(fields):
            share[step, q] = weight[q] * (scale * sums[q])
        couple = remote(step, COUPLE, share.at[step], flux.at[step], partner)
        couple.start()
        pending = pending + [(couple, None)]

        def inner(k, carry, **ends):
            interior(moment, k, src, dst, **ends)
            return carry

        split_at = levels - 1 if final else 2 + 2 * INNER
        levels_loop(2, split_at, inner, 0, INNER)
        if final:
            inner(levels - 1, 0, last=True)
        couple.wait_recv()
        for q in range(fields):
            src[q, 0] = src[q, 0] + (flux[step, q] - share[step, q])
        if not final:
            for copy in coeffs[moment - 1]:
                copy.wait()
            for side in (NORTH, SOUTH):
                row_local(moment, side, src)
                row_coefs(moment - 1, side)
                put_early(moment - 1, side, row_own[side])
            early = early_copies()
            start_rows(early)
            levels_loop(split_at, levels - 1, inner, 0, INNER)
            inner(levels - 1, 0, last=True)
        inner(0, 0, first=True)
        inner(1, 0)
        if not final:
            own_e, own_w = split(gather((zero, zero), dst, 0, levels))
            col_coefs(moment - 1)
            for side, r in ((NORTH, rows - 1), (SOUTH, 0)):
                for way, line in enumerate(col_corner(row_coef[2 * (moment - 1) + side])):
                    row_corner[side, way:way + 1] = line
                row_keep[side] = row_out[0, side, 0:slots]
                for q in range(fields):
                    at = slice(slot_of(q, 0), slot_of(q, 0) + 1)
                    row_keep[side, at] = row_coef[2 * moment + side, at] * src[q, 0, r:r + 1]

        wait_recv(early if final else row_halo)
        if final:
            receive_early()
        else:
            receive_rows(row_in)
        wait_recv(late)
        got_e, got_w = receive_cols(step)
        if final:
            got_e, got_w = receive_late(step, (got_e, got_w))
        else:
            add_shares(step, row_in)
            col_more = [col_corner(row_got[side]) for side in (NORTH, SOUTH)]
            col_sides = []
            for side, value in ((EAST, own_e + got_e), (WEST, own_w + got_w)):
                value = value + jnp.where(row == rows - 1, col_more[NORTH][side], 0.0)
                col_sides.append(value + jnp.where(row == 0, col_more[SOUTH][side], 0.0))
            put_cols(step + 1, moment - 1, col_sides)
            col_halo = col_copies(step + 1)
            start(col_halo)
            row_sides = [row_own[side] + row_got[side] for side in (NORTH, SOUTH)]
            put_sides(step + 1, col_sides, row_sides, (got_e, got_w))
            side_halo = side_copies(step + 1)
            start(side_halo)
            late = col_halo + side_halo
            pending = pending + early + late

        pair = joined(got_w, got_e)
        if final:
            pair_v[0], pair_v[1] = pair
            break

        sums = [zero] * fields
        for k in range(levels):
            for q in range(fields):
                total = finished(dst[q, k], pair[q // half], row_got, (q % half) * levels + k, slot_of(q, k))
                dst[q, k] = total
                sums[q] = sums[q] + jnp.where(k < depth[...], total, 0.0)

    for copy, go in pending:
        if go is None:
            copy.wait_send()
        else:
            pl.when(go)(copy.wait_send)


def solution(mesh):
    lats, lons = mesh.shape["lat"], mesh.shape["lon"]

    def shards(adjoint, land_mask, coupling_depth, coupling_weight, diffusion, velocity, mixing):
        _, fields, levels, rows, cols = adjoint.shape
        steps = diffusion.shape[0]
        f32 = jnp.float32
        block = (rows, cols)
        slots = fields * levels
        column = pltpu.VMEM((steps, 2, rows, cols), f32)
        edge = pltpu.VMEM((1, 2, slots + 8, cols), f32)
        early = pltpu.VMEM((1, 2, slots + 2 * levels, cols), f32)
        side_out, side_in = pltpu.VMEM((steps, 2, 8, cols), f32), pltpu.VMEM((steps, 2, 2, 8, cols), f32)
        parts = pl.pallas_call(
            functools.partial(kernel, lats, lons),
            out_shape=(
                jax.ShapeDtypeStruct(adjoint.shape, f32),
                jax.ShapeDtypeStruct((2, rows, cols), f32),
                jax.ShapeDtypeStruct((2, slots, cols), f32),
            ),
            in_specs=[pl.BlockSpec(memory_space=pltpu.HBM)] * 7,
            out_specs=(pl.BlockSpec(memory_space=pltpu.VMEM),) * 3,
            scratch_shapes=[
                pltpu.VMEM((fields, levels, rows, cols), f32),
                pltpu.VMEM((fields, levels, rows, cols), f32),
                pltpu.VMEM((steps, levels, rows, cols), f32),
                pltpu.VMEM((steps, 2, levels, rows, cols), f32),
                pltpu.VMEM((steps, levels, rows, cols), f32),
                pltpu.VMEM(block, jnp.int32),
                pltpu.VMEM(block, jnp.int32),
                pltpu.VMEM((fields, rows, cols), f32),
                pltpu.VMEM(block, f32),
                pltpu.VMEM((steps, fields, rows, cols), f32),
                pltpu.VMEM((steps, fields, rows, cols), f32),
                pltpu.VMEM((2, rows, cols), jnp.int32),
                pltpu.VMEM((2, rows, cols), f32),
                column,
                pltpu.VMEM((2, fields // 2, 8, cols), f32),
                pltpu.VMEM((steps * 2, slots, cols), f32),
                pltpu.VMEM((2, slots, cols), f32),
                pltpu.VMEM((2, slots, cols), f32),
                pltpu.VMEM((2, 8, cols), f32),
                early, early,
                column, column, side_out, side_in,
                edge, edge, side_out, side_in,
                pltpu.SemaphoreType.DMA((10 + 3 * steps,)),
                pltpu.SemaphoreType.DMA((steps, COPIES)),
                pltpu.SemaphoreType.DMA((steps, COPIES)),
            ],
            compiler_params=pltpu.CompilerParams(
                collective_id=0, has_side_effects=True, vmem_limit_bytes=40 * 1024 * 1024
            ),
            name="adjoint",
        )(*(pltpu.with_memory_space_constraint(x, pltpu.HBM) for x in (adjoint, land_mask, coupling_depth, coupling_weight, diffusion, velocity, mixing)))
        return pl.pallas_call(
            finish_kernel,
            out_shape=jax.ShapeDtypeStruct(adjoint.shape, f32),
            in_specs=[pl.BlockSpec(memory_space=pltpu.VMEM)] * 3,
            out_specs=pl.BlockSpec(memory_space=pltpu.HBM),
            scratch_shapes=[
                pltpu.VMEM((fields, levels, rows, cols), f32), pltpu.SemaphoreType.DMA((PIECES * fields,)),
            ],
            compiler_params=pltpu.CompilerParams(vmem_limit_bytes=16 * 1024 * 1024),
            name="adjoint_finish",
        )(*parts)

    in_specs = (
        P("ice", None, None, "lat", "lon"),
        P("lat", "lon"),
        P("ice", "lat", "lon"),
        P("ice", None, "lat", "lon"),
        P(None, "ice", None, "lat", "lon"),
        P(None, "ice", None, None, "lat", "lon"),
        P(None, "ice", None, "lat", "lon"),
    )
    out_specs = P("ice", None, None, "lat", "lon")
    return jax.shard_map(shards, mesh=mesh, in_specs=in_specs, out_specs=out_specs, check_vma=False)
```
